512 devices in a mesh: tm: 64 (over z, y), band: 8 (over x, core).
Axes of the slice: x: 4, y: 8, z: 8, core: 2. Of those that a mesh axis runs over, the one named last changes fastest.
Arguments:
- audio_clips: float32 [8, 2, 112896], P(None, None, 'tm'), may hold values from -6 to 6
- band_widths: int32 [64], replicated, may hold values from 1 to 128, 1024 in all
- band_gain: float32 [64, 512], P('band'), may hold values from 0.25 to 1.75
- band_weight: bfloat16 [64, 512, 384], P('band', 'tm'), may hold values from -0.5 to 0.5
- norm_gain: float32 [384], replicated, may hold values from 0.25 to 1.75
- qkv_weight: bfloat16 [384, 1536], replicated
- out_weight: bfloat16 [512, 384], replicated, may hold values from -0.25 to 0.25
- cotangent: bfloat16 [64, 8, 256, 384], P('band', None, 'tm'), may hold values from -6 to 6
Outputs:
- attended: bfloat16 [64, 8, 256, 384], P('band', None, 'tm')
- grad_qkv: float32 [384, 1536], replicated
- grad_out: float32 [512, 384], replicated
The draws below stay inside these ranges and needn't reach their ends.
Inputs may be any that keep to these rules, and one draw needn't show every extreme that they name: `band_widths`: the bands are consecutive and cover all 1024 bins; the widest has exactly 128 bins.
All inputs are finite; a program needn't handle non-finite values.
Results may differ from the reference program's by a relative error of at most 0.0095.
Values may be sent and summed in bfloat16 or wider, within the bound.
No kernel may reach another device: no remote copies, remote signals or barrier semaphores. Data moves between devices by JAX's collectives and lax.ppermute only.
A program may use at most 64 MiB of HBM per device.

```python
import math
import jax
import jax.numpy as jnp
import numpy as np
from jax import lax

D = 384
HEADS = 8
HDIM = 64
WIN = 2048
HOP = 441
BANDS = 64
MAXW = 128
CLIPS = 8
INNER = 512
BINS = 1024
FEAT = 512
FRAMES = 256
SAMPLES = 112896


def draw_qkv_weight(key, part):
    drawn_draw = jax.random.normal(key, (D, 3 * INNER), jnp.float32) * D ** (-0.5)
    return drawn_draw.astype(jnp.bfloat16)


def block_levels(rng, extent, pieces, least, top_value):
    factor_of = 1.0
    for dim, shards_of in pieces:
        steps = jax.random.uniform(jax.random.fold_in(jax.random.fold_in(rng, 6), dim), (shards_of,), jnp.float32, least / len(pieces), top_value / len(pieces))
        factor_of = factor_of * jnp.repeat(jnp.exp(steps), extent[dim] // shards_of).reshape((-1,) + (1,) * (len(extent) - 1 - dim))
    return factor_of


def length_profile(number_of, total, most, lean):
    loads = [(1 << 20) // math.isqrt(rank ** lean) + 1 for rank in range(2, number_of + 1)]
    rest, given = total - most - (number_of - 1), [1] * (number_of - 1)
    while rest > 0:
        candidates = [i for i in range(number_of - 1) if given[i] < most]
        mass, left = sum([loads[i] for i in candidates]), rest
        for i in candidates:
            extra = min(most - given[i], max(1, left * loads[i] // mass), rest)
            given[i] = given[i] + extra
            rest = rest - extra
    return np.array([most] + given)


def ragged(own_key, count, total, most, skew):
    if count == 2:
        one = jax.random.randint(own_key, (), max(1, total - most), min(most, total - 1) + 1)
        return jnp.stack([one, total - one])
    lengths = jnp.asarray(length_profile(count, total, most, skew), jnp.int32)
    couples = (count - 1) // 2
    donor, receiver = lengths[1:1 + 2 * couples:2], lengths[2:2 + 2 * couples:2]
    room = jnp.minimum(donor - 1, most - receiver)
    shifted = jax.random.randint(jax.random.fold_in(own_key, 1), (couples,), 0, 1 << 20) % (room + 1)
    lengths = lengths.at[1:1 + 2 * couples:2].set(donor - shifted).at[2:2 + 2 * couples:2].set(receiver + shifted)
    return lengths[jax.random.permutation(jax.random.fold_in(own_key, 2), count)]


def centred(stream_key, dims, scale, most, split=(), kind=jnp.bfloat16):
    factor_of = block_levels(stream_key, dims, split, -0.22, 0.18) if split else 1.0
    entries = jax.random.normal(stream_key, dims, jnp.float32) * scale * factor_of
    return jnp.minimum(jnp.maximum(entries, -most), most).astype(kind)


def setup_inputs(seed: int = 0) -> dict:
    arg_keys = jax.random.split(jax.random.key(seed), 9)
    return {
        "audio_clips": centred(arg_keys[0], (CLIPS, 2, SAMPLES), 1.0, 6.0, ((2, 64),), jnp.float32),
        "band_widths": ragged(arg_keys[1], BANDS, BINS, MAXW, 2).astype(jnp.int32),
        "band_gain": jnp.clip(1.0 + 0.15 * jax.random.normal(arg_keys[2], (BANDS, FEAT), jnp.float32), 0.25, 1.75),
        "band_weight": centred(arg_keys[3], (BANDS, FEAT, D), (FEAT // 4) ** -0.5, 0.5, ((0, 8), (1, 64))),
        "norm_gain": jnp.clip(1.0 + 0.15 * jax.random.normal(arg_keys[4], (D,), jnp.float32), 0.25, 1.75),
        "qkv_weight": draw_qkv_weight(jax.random.fold_in(arg_keys[8], 71), 0),
        "out_weight": centred(arg_keys[6], (INNER, D), INNER ** -0.5, 0.25),
        "cotangent": centred(arg_keys[7], (BANDS, CLIPS, FRAMES, D), 1.0, 6.0, ((0, 8), (2, 64))),
    }


def dft_table(window_len, first_bin, bin_count):
    sample_at = lax.iota(jnp.int32, window_len)
    bin_at = first_bin + lax.iota(jnp.int32, bin_count)
    phase = sample_at[:, None] * bin_at[None, :] % window_len
    angle = phase.astype(jnp.float32) * (2.0 * math.pi / window_len)
    taper = 0.5 - 0.5 * jnp.cos(sample_at.astype(jnp.float32) * (2.0 * math.pi / window_len))
    column = (taper / math.sqrt(window_len))[:, None]
    return jnp.stack([jnp.cos(angle) * column, -jnp.sin(angle) * column], axis=1)

def cut_frames(samples, frame_total, hop_len, window_len):
    position = lax.iota(jnp.int32, frame_total)[:, None] * hop_len + lax.iota(jnp.int32, window_len)[None, :]
    return jnp.take(samples, position, axis=2)

def band_normed(raw, band_width, gain_row):
    keep_bins = (lax.iota(jnp.int32, MAXW) < band_width).astype(jnp.float32)
    masked = raw * keep_bins
    mean_sq = lax.optimization_barrier(jnp.sum(masked * masked, axis=(1, 3, 4))) / (4 * band_width).astype(jnp.float32)
    inverse = lax.rsqrt(jnp.maximum(mean_sq, 0.25))
    scaled = masked * inverse[:, None, :, None, None]
    arranged = jnp.transpose(scaled, (0, 2, 4, 1, 3)).reshape(-1, FEAT)
    return (arranged * gain_row[None, :]).astype(jnp.bfloat16)

def rotary_tables(frame_total):
    position = lax.iota(jnp.int32, frame_total).astype(jnp.float32)
    freq = jnp.exp(lax.iota(jnp.int32, HDIM // 2).astype(jnp.float32) * (-2.0 * math.log(10000.0) / HDIM))
    angle = position[:, None] * freq[None, :]
    return (jnp.cos(angle)[:, None, :], jnp.sin(angle)[:, None, :])

def rotate(values, cosine, sine_part, sign):
    first_half = values[..., :HDIM // 2]
    second_half = values[..., HDIM // 2:]
    return jnp.concatenate([first_half * cosine - sign * second_half * sine_part, second_half * cosine + sign * first_half * sine_part], axis=-1)

def layer(x_seq, g_seq, norm_gain, qkv_weight, out_weight, product):
    frame_total = x_seq.shape[0]
    x_full = x_seq.astype(jnp.float32)
    normed_x = (x_full * lax.rsqrt(lax.optimization_barrier(jnp.mean(x_full * x_full, axis=-1, keepdims=True)) + 1e-06) * norm_gain).astype(jnp.bfloat16)
    projected = product('fd,de->fe', normed_x, qkv_weight)
    query = projected[:, :INNER].reshape(frame_total, HEADS, HDIM)
    key_part = projected[:, INNER:2 * INNER].reshape(frame_total, HEADS, HDIM)
    value_part = projected[:, 2 * INNER:].reshape(frame_total, HEADS, HDIM)
    cosine, sine_part = rotary_tables(frame_total)
    factor = 1.0 / math.sqrt(HDIM)
    query_b = (rotate(query, cosine, sine_part, 1.0) * factor).astype(jnp.bfloat16)
    key_b = rotate(key_part, cosine, sine_part, 1.0).astype(jnp.bfloat16)
    value_b = value_part.astype(jnp.bfloat16)
    grad_mixed = product('fd,id->fi', g_seq, out_weight).astype(jnp.bfloat16).reshape(frame_total, HEADS, HDIM)

    def head_pass(operands):
        head_q, head_k, head_v, head_g = operands
        scores = product('fd,gd->fg', head_q, head_k)
        peak = lax.optimization_barrier(jnp.max(scores, axis=-1, keepdims=True))
        expo = jnp.exp(scores - peak)
        probs = expo / lax.optimization_barrier(jnp.sum(expo, axis=-1, keepdims=True))
        probs_b = probs.astype(jnp.bfloat16)
        mixed = product('fg,gd->fd', probs_b, head_v)
        grad_p = product('fd,gd->fg', head_g, head_v)
        grad_v = product('fg,fd->gd', probs_b, head_g)
        row_dot = lax.optimization_barrier(jnp.sum(probs * grad_p, axis=-1, keepdims=True))
        grad_s = (probs * (grad_p - row_dot)).astype(jnp.bfloat16)
        grad_q = product('fg,gd->fd', grad_s, head_k)
        grad_k = product('fg,fd->gd', grad_s, head_q)
        return (mixed, grad_q, grad_k, grad_v)

    def heads_first(values):
        return jnp.transpose(values, (1, 0, 2))
    mixed, grad_q, grad_k, grad_v = lax.map(head_pass, (heads_first(query_b), heads_first(key_b), heads_first(value_b), heads_first(grad_mixed)))
    mixed_b = heads_first(mixed).reshape(frame_total, INNER).astype(jnp.bfloat16)
    attended = (x_full + product('fi,id->fd', mixed_b, out_weight)).astype(jnp.bfloat16)
    grad_out = product('fi,fd->id', mixed_b, g_seq)
    grad_query = rotate(heads_first(grad_q) * factor, cosine, sine_part, -1.0).reshape(frame_total, INNER)
    grad_key = rotate(heads_first(grad_k), cosine, sine_part, -1.0).reshape(frame_total, INNER)
    grad_value = heads_first(grad_v).reshape(frame_total, INNER)
    grad_proj = jnp.concatenate([grad_query, grad_key, grad_value], axis=-1).astype(jnp.bfloat16)
    grad_qkv = product('fd,fe->de', normed_x, grad_proj)
    return (attended, grad_qkv, grad_out)

def exact_product(pattern, left, right):
    return jnp.einsum(pattern, left.astype(jnp.float32), right.astype(jnp.float32))

def reference(audio_clips, band_widths, band_gain, band_weight, norm_gain, qkv_weight, out_weight, cotangent):
    padded = jnp.concatenate([audio_clips, jnp.zeros((CLIPS, 2, WIN - HOP), audio_clips.dtype)], axis=2)
    frames = cut_frames(padded, FRAMES, HOP, WIN)
    spectrum = jnp.einsum('cafn,nrk->cafrk', frames, dft_table(WIN, 0, BINS), precision=lax.Precision.HIGHEST)
    starts = (jnp.cumsum(band_widths, dtype=jnp.int32) - band_widths).astype(jnp.int32)

    def embed_band(inputs_now):
        band_width, row_start, gain_row, weight_rows = inputs_now
        bin_index = jnp.clip(row_start + lax.iota(jnp.int32, MAXW), 0, BINS - 1).astype(jnp.int32)
        raw = jnp.take(spectrum, bin_index, axis=4)
        normed = band_normed(raw, band_width, gain_row)
        return jnp.dot(normed, weight_rows, preferred_element_type=jnp.float32).astype(jnp.bfloat16)
    tokens = lax.map(embed_band, (band_widths, starts, band_gain, band_weight))
    sequences = tokens.reshape(BANDS * CLIPS, FRAMES, D)
    cotangents = cotangent.reshape(BANDS * CLIPS, FRAMES, D)

    def advance(totals, seq_pair):
        attended, grad_qkv, grad_out = layer(seq_pair[0], seq_pair[1], norm_gain, qkv_weight, out_weight, exact_product)
        return ((totals[0] + grad_qkv, totals[1] + grad_out), attended)
    start_totals = (jnp.zeros((D, 3 * INNER), jnp.float32), jnp.zeros((INNER, D), jnp.float32))
    totals, attended = lax.scan(advance, start_totals, (sequences, cotangents))
    factor_all = 1.0 / math.sqrt(BANDS * CLIPS * FRAMES)
    return (attended.reshape(BANDS, CLIPS, FRAMES, D), totals[0] * factor_all, totals[1] * factor_all)
```

```python
import math

import jax
import jax.numpy as jnp
import numpy as np
from jax import lax
from jax.experimental import pallas as pl
from jax.experimental.pallas import tpu as pltpu
from jax.sharding import Mesh, PartitionSpec as P

D = 384
HEADS = 8
HDIM = 64
WIN = 2048
HOP = 441
BANDS = 64
MAXW = 128
CLIPS = 8
INNER = 512
BINS = 1024
FEAT = 512
FRAMES = 256

OUTER = 8
SPAN = WIN // OUTER
HIGH = BINS // OUTER


def window_table():
    sample_at = np.arange(WIN, dtype=np.float64)
    taper = (0.5 - 0.5 * np.cos(sample_at * (2.0 * np.pi / WIN))) / np.sqrt(WIN)
    return taper.reshape(1, WIN).astype(np.float32)


def twiddle_table():
    phase = np.outer(np.arange(OUTER), np.arange(SPAN)) % WIN
    angle = phase * (2.0 * np.pi / WIN)
    return np.concatenate([np.cos(angle), np.sin(angle)], axis=0).astype(np.float32)


def inner_table():
    phase = np.outer(np.arange(SPAN), np.arange(HIGH)) % SPAN
    angle = phase * (2.0 * np.pi / SPAN)
    real, imag = np.cos(angle), np.sin(angle)
    return np.concatenate(
        [np.concatenate([real, -imag], axis=1), np.concatenate([imag, real], axis=1)], axis=0
    ).astype(np.float32)


def rotary_table(frame_order):
    freq = np.exp(np.arange(HDIM // 2, dtype=np.float32) * np.float32(-2.0 * math.log(10000.0) / HDIM))
    angle = (frame_order.astype(np.float32)[:, None] * freq.astype(np.float32)[None, :]).astype(np.float64)
    cosine, sine = np.cos(angle), np.sin(angle)
    return (
        np.concatenate([cosine] * 4, axis=1).astype(np.float32),
        np.concatenate([-sine, sine, -sine, sine], axis=1).astype(np.float32),
    )


def spectrum_kernel(
    frames_here,
    widths_ref,
    starts_ref,
    audio_ref,
    rim_ref,
    gain_ref,
    place_ref,
    taper_ref,
    twiddle_ref,
    inner_ref,
    out_ref,
    lead,
    tail,
    framed,
    stage,
    bins,
    pick,
):
    own = audio_ref.shape[1]
    rows = audio_ref.shape[0]
    total = rows * frames_here
    lead[:, :own] = audio_ref[...]
    tail[:, : WIN - HOP] = rim_ref[...]
    lane = lax.broadcasted_iota(jnp.int32, (rows, WIN), 1)
    for f in range(frames_here):
        here = own - HOP * f
        head = lead[...] if f == 0 else pltpu.roll(lead[...], WIN - HOP * f, 1)
        rest = pltpu.roll(tail[...], here % WIN, 1)
        frame = jnp.where(lane < here, head, rest) * taper_ref[...]
        for block in range(WIN // 128):
            framed[block, pl.ds(f, rows, stride=frames_here), :] = frame[
                :, block * 128 : (block + 1) * 128
            ]
    root = math.sqrt(0.5)
    for half in range(SPAN // 128):
        x = [framed[2 * n + half] for n in range(OUTER)]
        e0, e1, e2, e3 = x[0] + x[4], x[1] + x[5], x[2] + x[6], x[3] + x[7]
        d0, d1, d2, d3 = x[0] - x[4], x[1] - x[5], x[2] - x[6], x[3] - x[7]
        s02, s13 = e0 + e2, e1 + e3
        p = (d1 - d3) * root
        q = (d1 + d3) * root
        real = [s02 + s13, d0 + p, e0 - e2, d0 - p, s02 - s13]
        imag = [None, -(q + d2), e3 - e1, d2 - q, None]
        lanes = slice(half * 128, (half + 1) * 128)
        for low in range(OUTER):
            if low <= 4:
                re, im = real[low], imag[low]
            else:
                re, im = real[8 - low], -imag[8 - low]
            at = slice(low * total, (low + 1) * total)
            if low == 0:
                stage[at, half * 128 : (half + 1) * 128] = re
                stage[at, SPAN + half * 128 : SPAN + (half + 1) * 128] = jnp.zeros_like(re)
                continue
            c = twiddle_ref[low : low + 1, lanes]
            s = twiddle_ref[OUTER + low : OUTER + low + 1, lanes]
            if im is None:
                zr, zi = re * c, -(re * s)
            else:
                zr, zi = re * c + im * s, im * c - re * s
            stage[at, half * 128 : (half + 1) * 128] = zr
            stage[at, SPAN + half * 128 : SPAN + (half + 1) * 128] = zi
    made = jnp.dot(
        stage[...],
        inner_ref[...],
        preferred_element_type=jnp.float32,
        precision=lax.Precision.HIGHEST,
    )
    for low in range(OUTER):
        for part in range(2):
            piece = made[low * total : (low + 1) * total, part * HIGH : (part + 1) * HIGH]
            cols = slice(low * HIGH, (low + 1) * HIGH)
            for split in range(3):
                at = (split * 2 + part) * total
                kept = piece.astype(jnp.bfloat16)
                bins[at : at + total, cols] = kept
                piece = piece - kept.astype(jnp.float32)
    target = place_ref[...]
    for low in range(OUTER):
        bin_at = low + OUTER * lax.broadcasted_iota(jnp.int32, (HIGH, target.shape[1]), 0)
        pick[low * HIGH : (low + 1) * HIGH, :] = jnp.where(bin_at == target, 1.0, 0.0).astype(
            jnp.bfloat16
        )
    own_bands = target.shape[1] // MAXW
    half_rows = total // 2
    chosen = jnp.dot(bins[...], pick[...], preferred_element_type=jnp.float32)
    exact = chosen[: 2 * total] + chosen[2 * total : 4 * total] + chosen[4 * total :]
    for band in range(own_bands):
        cols = slice(band * MAXW, (band + 1) * MAXW)
        re = exact[:total, cols]
        im = exact[total:, cols]
        power = jnp.sum(re * re + im * im, axis=1, keepdims=True)
        power = power[:half_rows] + power[half_rows:]
        count = (4 * widths_ref[0, band]).astype(jnp.float32)
        inverse = lax.rsqrt(jnp.maximum(power / count, 0.25))
        for a in range(2):
            for r in range(2):
                value = (re, im)[r][a * half_rows : (a + 1) * half_rows]
                which = 2 * a + r
                out_ref[
                    band * half_rows : (band + 1) * half_rows,
                    which * MAXW : (which + 1) * MAXW,
                ] = (value * inverse * gain_ref[band, which : which + 1, :]).astype(jnp.bfloat16)


def swap_halves(values):
    width = values.shape[1]
    lane = lax.broadcasted_iota(jnp.int32, values.shape, 1)
    forward = pltpu.roll(values, width - HDIM // 2, 1)
    backward = pltpu.roll(values, HDIM // 2, 1)
    return jnp.where(lane % HDIM < HDIM // 2, forward, backward)


def dot(left, right, dims=((1,), (0,))):
    return lax.dot_general(left, right, (dims, ((), ())), preferred_element_type=jnp.float32)


def layer_kernel(
    feats_ref,
    weight_ref,
    grads_ref,
    gain_ref,
    qkv_ref,
    outw_ref,
    cos_ref,
    sin_ref,
    attended_ref,
    grad_qkv_ref,
    grad_out_ref,
    query_s,
    key_s,
    mixed_s,
    gproj_s,
    *,
    factor_all,
):
    natural = lax.broadcasted_iota(jnp.int32, (FEAT, FEAT), 1)
    wanted = lax.broadcasted_iota(jnp.int32, (FEAT, FEAT), 0)
    wanted = (wanted % MAXW) * 4 + wanted // MAXW
    order = jnp.where(natural == wanted, 1.0, 0.0).astype(jnp.bfloat16)
    weight = dot(order, weight_ref[...]).astype(jnp.bfloat16)
    x = dot(feats_ref[...], weight).astype(jnp.bfloat16).astype(jnp.float32)
    scale = lax.rsqrt(jnp.mean(x * x, axis=1, keepdims=True) + 1e-06)
    normed_x = (x * scale * gain_ref[...]).astype(jnp.bfloat16)
    factor = 1.0 / math.sqrt(HDIM)
    cosine = cos_ref[...]
    sine = sin_ref[...]
    qk = dot(normed_x, qkv_ref[:, : 2 * INNER])
    for block in range(INNER // 128):
        cols = slice(block * 128, (block + 1) * 128)
        q = qk[:, cols]
        k = qk[:, INNER + block * 128 : INNER + (block + 1) * 128]
        query_s[:, cols] = ((q * cosine + swap_halves(q) * sine) * factor).astype(jnp.bfloat16)
        key_s[:, cols] = (k * cosine + swap_halves(k) * sine).astype(jnp.bfloat16)
    value_b = dot(normed_x, qkv_ref[:, 2 * INNER :]).astype(jnp.bfloat16)
    grad_mixed = dot(grads_ref[...], outw_ref[...], ((1,), (1,))).astype(jnp.bfloat16)
    for pair in range(HEADS // 2):
        cols = slice(pair * 128, (pair + 1) * 128)
        results = []
        for side in range(2):
            head = slice(side * HDIM, (side + 1) * HDIM)
            head_q = query_s[:, cols][:, head]
            head_k = key_s[:, cols][:, head]
            head_v = value_b[:, cols][:, head]
            head_g = grad_mixed[:, cols][:, head]
            scores = dot(head_q, head_k, ((1,), (1,)))
            peak = jnp.max(scores, axis=1, keepdims=True)
            expo = jnp.exp(scores - peak)
            probs = expo / jnp.sum(expo, axis=1, keepdims=True)
            probs_b = probs.astype(jnp.bfloat16)
            mixed = dot(probs_b, head_v)
            grad_p = dot(head_g, head_v, ((1,), (1,)))
            grad_v = dot(probs_b, head_g, ((0,), (0,)))
            row_dot = jnp.sum(probs * grad_p, axis=1, keepdims=True)
            grad_s = (probs * (grad_p - row_dot)).astype(jnp.bfloat16)
            grad_q = dot(grad_s, head_k)
            grad_k = dot(grad_s, head_q, ((0,), (0,)))
            results.append((mixed, grad_q, grad_k, grad_v))
        mixed, grad_q, grad_k, grad_v = (
            jnp.concatenate([low, high], axis=1) for low, high in zip(*results)
        )
        mixed_s[:, cols] = mixed.astype(jnp.bfloat16)
        grad_q = grad_q * factor
        gproj_s[:, cols] = (grad_q * cosine - swap_halves(grad_q) * sine).astype(jnp.bfloat16)
        gproj_s[:, INNER + pair * 128 : INNER + (pair + 1) * 128] = (
            grad_k * cosine - swap_halves(grad_k) * sine
        ).astype(jnp.bfloat16)
        gproj_s[:, 2 * INNER + pair * 128 : 2 * INNER + (pair + 1) * 128] = grad_v.astype(
            jnp.bfloat16
        )
    mixed_b = mixed_s[...]
    attended_ref[...] = (x + dot(mixed_b, outw_ref[...])).astype(jnp.bfloat16)
    grad_out_ref[...] = (dot(mixed_b, grads_ref[...], ((0,), (0,))) * factor_all).astype(
        grad_out_ref.dtype
    )
    grad_qkv_ref[...] = (dot(normed_x, gproj_s[...], ((0,), (0,))) * factor_all).astype(
        grad_qkv_ref.dtype
    )


def whole(memory_space=pltpu.VMEM):
    return pl.BlockSpec(memory_space=memory_space)


def spectrum(frames_here, widths_own, starts_own, audio, rim, gain, place):
    rows, own = audio.shape
    total = rows * frames_here
    own_bands = place.shape[1] // MAXW
    return pl.pallas_call(
        lambda *refs: spectrum_kernel(frames_here, *refs),
        out_shape=jax.ShapeDtypeStruct((own_bands * total // 2, FEAT), jnp.bfloat16),
        in_specs=[whole(pltpu.SMEM)] * 2 + [whole()] * 7,
        out_specs=whole(),
        scratch_shapes=[
            pltpu.VMEM((rows, WIN), jnp.float32),
            pltpu.VMEM((rows, WIN), jnp.float32),
            pltpu.VMEM((WIN // 128, total, 128), jnp.float32),
            pltpu.VMEM((OUTER * total, 2 * SPAN), jnp.float32),
            pltpu.VMEM((6 * total, BINS), jnp.bfloat16),
            pltpu.VMEM((BINS, own_bands * MAXW), jnp.bfloat16),
        ],
        name="spectrum",
    )(
        widths_own,
        starts_own,
        audio,
        rim,
        gain,
        place,
        jnp.asarray(window_table()),
        jnp.asarray(twiddle_table()),
        jnp.asarray(inner_table()),
    )


def layer(feats, weight, grads, norm_gain, qkv_weight, out_weight, factor_all, grad_type):
    cosine, sine = rotary_table(np.arange(FRAMES))
    return pl.pallas_call(
        lambda *refs: layer_kernel(*refs, factor_all=factor_all),
        out_shape=(
            jax.ShapeDtypeStruct((FRAMES, D), jnp.bfloat16),
            jax.ShapeDtypeStruct((D, 3 * INNER), grad_type),
            jax.ShapeDtypeStruct((INNER, D), grad_type),
        ),
        in_specs=[whole()] * 8,
        out_specs=(whole(),) * 3,
        scratch_shapes=[
            pltpu.VMEM((FRAMES, INNER), jnp.bfloat16),
            pltpu.VMEM((FRAMES, INNER), jnp.bfloat16),
            pltpu.VMEM((FRAMES, INNER), jnp.bfloat16),
            pltpu.VMEM((FRAMES, 3 * INNER), jnp.bfloat16),
        ],
        name="layer",
    )(
        feats,
        weight,
        grads,
        norm_gain.reshape(1, D),
        qkv_weight,
        out_weight,
        jnp.asarray(cosine),
        jnp.asarray(sine),
    )


def body(
    audio_clips, band_widths, band_gain, band_weight, norm_gain, qkv_weight, out_weight, cotangent
):
    tm = lax.axis_size("tm")
    own_bands = BANDS // lax.axis_size("band")
    frame_block = audio_clips.shape[2] // HOP
    audio = jnp.transpose(audio_clips, (1, 0, 2)).reshape(2 * CLIPS, -1)
    rim = lax.ppermute(
        audio[:, : WIN - HOP], "tm", [(source, source - 1) for source in range(1, tm)]
    )
    starts = jnp.cumsum(band_widths, dtype=jnp.int32) - band_widths
    first_band = lax.axis_index("band") * own_bands
    widths_own = lax.dynamic_slice_in_dim(band_widths, first_band, own_bands)
    starts_own = lax.dynamic_slice_in_dim(starts, first_band, own_bands)
    within = lax.iota(jnp.int32, MAXW)[None, :]
    place = jnp.where(within < widths_own[:, None], starts_own[:, None] + within, -1)
    gain = jnp.transpose(band_gain.reshape(own_bands, MAXW, 4), (0, 2, 1))
    normed = spectrum(
        frame_block,
        widths_own.reshape(1, own_bands),
        starts_own.reshape(1, own_bands),
        audio,
        rim,
        gain,
        place.reshape(1, own_bands * MAXW),
    )
    sequences = own_bands * CLIPS
    early = jnp.concatenate(
        [
            cotangent.reshape(sequences, frame_block, D),
            jnp.broadcast_to(
                band_weight[:, None], (own_bands, CLIPS, FEAT // tm, D)
            ).reshape(sequences, FEAT // tm, D),
        ],
        axis=1,
    )
    early = lax.all_to_all(early, "tm", split_axis=0, concat_axis=0, tiled=True)
    grads = early[:, :frame_block].reshape(FRAMES, D)
    weight = early[:, frame_block:].reshape(FEAT, D)
    feats = lax.all_to_all(
        normed.reshape(sequences, frame_block, FEAT), "tm", split_axis=0, concat_axis=0, tiled=True
    ).reshape(FRAMES, FEAT)
    factor_all = 1.0 / math.sqrt(BANDS * CLIPS * FRAMES)
    attended, grad_qkv, grad_out = layer(
        feats, weight, grads, norm_gain, qkv_weight, out_weight, factor_all, jnp.float32
    )
    returned = lax.all_to_all(
        attended.reshape(tm, frame_block, D), "tm", split_axis=0, concat_axis=0, tiled=True
    )
    attended_out = returned.reshape(own_bands, CLIPS, frame_block, D)
    grad_qkv, grad_out = lax.psum((grad_qkv, grad_out), ("tm", "band"))
    return (attended_out, grad_qkv, grad_out)


def solution(mesh):
    return jax.shard_map(
        body,
        mesh=mesh,
        in_specs=(
            P(None, None, "tm"),
            P(),
            P("band", None),
            P("band", "tm", None),
            P(),
            P(),
            P(),
            P("band", None, "tm", None),
        ),
        out_specs=(P("band", None, "tm", None), P(), P()),
        check_vma=False,
    )
```

```python
import math

import jax
import jax.numpy as jnp
import numpy as np
from jax import lax
from jax.experimental import pallas as pl
from jax.experimental.pallas import tpu as pltpu
from jax.sharding import Mesh, PartitionSpec as P

D = 384
HEADS = 8
HDIM = 64
WIN = 2048
HOP = 441
BANDS = 64
MAXW = 128
CLIPS = 8
INNER = 512
BINS = 1024
FEAT = 512
FRAMES = 256

OUTER = 8
SPAN = WIN // OUTER
HIGH = BINS // OUTER


def window_table():
    sample_at = np.arange(WIN, dtype=np.float64)
    taper = (0.5 - 0.5 * np.cos(sample_at * (2.0 * np.pi / WIN))) / np.sqrt(WIN)
    return taper.reshape(1, WIN).astype(np.float32)


def twiddle_table():
    phase = np.outer(np.arange(OUTER), np.arange(SPAN)) % WIN
    angle = phase * (2.0 * np.pi / WIN)
    return np.concatenate([np.cos(angle), np.sin(angle)], axis=0).astype(np.float32)


def inner_table():
    phase = np.outer(np.arange(SPAN), np.arange(HIGH)) % SPAN
    angle = phase * (2.0 * np.pi / SPAN)
    real, imag = np.cos(angle), np.sin(angle)
    return np.concatenate(
        [np.concatenate([real, -imag], axis=1), np.concatenate([imag, real], axis=1)], axis=0
    ).astype(np.float32)


def rotary_table(frame_order):
    freq = np.exp(np.arange(HDIM // 2, dtype=np.float32) * np.float32(-2.0 * math.log(10000.0) / HDIM))
    angle = (frame_order.astype(np.float32)[:, None] * freq.astype(np.float32)[None, :]).astype(np.float64)
    cosine, sine = np.cos(angle), np.sin(angle)
    return (
        np.concatenate([cosine] * 4, axis=1).astype(np.float32),
        np.concatenate([-sine, sine, -sine, sine], axis=1).astype(np.float32),
    )


def spectrum_kernel(
    frames_here,
    widths_ref,
    starts_ref,
    audio_ref,
    rim_ref,
    gain_ref,
    place_ref,
    taper_ref,
    twiddle_ref,
    inner_ref,
    out_ref,
    lead,
    tail,
    framed,
    stage,
    bins,
    pick,
):
    own = audio_ref.shape[1]
    rows = audio_ref.shape[0]
    total = rows * frames_here
    lead[:, :own] = audio_ref[...]
    tail[:, : WIN - HOP] = rim_ref[...]
    lane = lax.broadcasted_iota(jnp.int32, (rows, WIN), 1)
    for f in range(frames_here):
        here = own - HOP * f
        head = lead[...] if f == 0 else pltpu.roll(lead[...], WIN - HOP * f, 1)
        rest = pltpu.roll(tail[...], here % WIN, 1)
        frame = jnp.where(lane < here, head, rest) * taper_ref[...]
        for block in range(WIN // 128):
            framed[block, pl.ds(f, rows, stride=frames_here), :] = frame[
                :, block * 128 : (block + 1) * 128
            ]
    root = math.sqrt(0.5)
    for half in range(SPAN // 128):
        x = [framed[2 * n + half] for n in range(OUTER)]
        e0, e1, e2, e3 = x[0] + x[4], x[1] + x[5], x[2] + x[6], x[3] + x[7]
        d0, d1, d2, d3 = x[0] - x[4], x[1] - x[5], x[2] - x[6], x[3] - x[7]
        s02, s13 = e0 + e2, e1 + e3
        p = (d1 - d3) * root
        q = (d1 + d3) * root
        real = [s02 + s13, d0 + p, e0 - e2, d0 - p, s02 - s13]
        imag = [None, -(q + d2), e3 - e1, d2 - q, None]
        lanes = slice(half * 128, (half + 1) * 128)
        for low in range(OUTER):
            if low <= 4:
                re, im = real[low], imag[low]
            else:
                re, im = real[8 - low], -imag[8 - low]
            at = slice(low * total, (low + 1) * total)
            if low == 0:
                stage[at, half * 128 : (half + 1) * 128] = re
                stage[at, SPAN + half * 128 : SPAN + (half + 1) * 128] = jnp.zeros_like(re)
                continue
            c = twiddle_ref[low : low + 1, lanes]
            s = twiddle_ref[OUTER + low : OUTER + low + 1, lanes]
            if im is None:
                zr, zi = re * c, -(re * s)
            else:
                zr, zi = re * c + im * s, im * c - re * s
            stage[at, half * 128 : (half + 1) * 128] = zr
            stage[at, SPAN + half * 128 : SPAN + (half + 1) * 128] = zi
    made = jnp.dot(
        stage[...],
        inner_ref[...],
        preferred_element_type=jnp.float32,
        precision=lax.Precision.HIGHEST,
    )
    for low in range(OUTER):
        for part in range(2):
            piece = made[low * total : (low + 1) * total, part * HIGH : (part + 1) * HIGH]
            cols = slice(low * HIGH, (low + 1) * HIGH)
            for split in range(3):
                at = (split * 2 + part) * total
                kept = piece.astype(jnp.bfloat16)
                bins[at : at + total, cols] = kept
                piece = piece - kept.astype(jnp.float32)
    target = place_ref[...]
    for low in range(OUTER):
        bin_at = low + OUTER * lax.broadcasted_iota(jnp.int32, (HIGH, target.shape[1]), 0)
        pick[low * HIGH : (low + 1) * HIGH, :] = jnp.where(bin_at == target, 1.0, 0.0).astype(
            jnp.bfloat16
        )
    own_bands = target.shape[1] // MAXW
    half_rows = total // 2
    chosen = jnp.dot(bins[...], pick[...], preferred_element_type=jnp.float32)
    exact = chosen[: 2 * total] + chosen[2 * total : 4 * total] + chosen[4 * total :]
    for band in range(own_bands):
        cols = slice(band * MAXW, (band + 1) * MAXW)
        re = exact[:total, cols]
        im = exact[total:, cols]
        power = jnp.sum(re * re + im * im, axis=1, keepdims=True)
        power = power[:half_rows] + power[half_rows:]
        count = (4 * widths_ref[0, band]).astype(jnp.float32)
        inverse = lax.rsqrt(jnp.maximum(power / count, 0.25))
        for a in range(2):
            for r in range(2):
                value = (re, im)[r][a * half_rows : (a + 1) * half_rows]
                which = 2 * a + r
                out_ref[
                    band * half_rows : (band + 1) * half_rows,
                    which * MAXW : (which + 1) * MAXW,
                ] = (value * inverse * gain_ref[band, which : which + 1, :]).astype(jnp.bfloat16)


def swap_halves(values):
    width = values.shape[1]
    lane = lax.broadcasted_iota(jnp.int32, values.shape, 1)
    forward = pltpu.roll(values, width - HDIM // 2, 1)
    backward = pltpu.roll(values, HDIM // 2, 1)
    return jnp.where(lane % HDIM < HDIM // 2, forward, backward)


def dot(left, right, dims=((1,), (0,))):
    return lax.dot_general(left, right, (dims, ((), ())), preferred_element_type=jnp.float32)


def layer_kernel(
    feats_ref,
    weight_ref,
    grads_ref,
    gain_ref,
    qkv_ref,
    outw_ref,
    cos_ref,
    sin_ref,
    attended_ref,
    partial_ref,
    query_s,
    key_s,
    mixed_s,
    gproj_s,
    *,
    factor_all,
):
    natural = lax.broadcasted_iota(jnp.int32, (FEAT, FEAT), 1)
    wanted = lax.broadcasted_iota(jnp.int32, (FEAT, FEAT), 0)
    wanted = (wanted % MAXW) * 4 + wanted // MAXW
    order = jnp.where(natural == wanted, 1.0, 0.0).astype(jnp.bfloat16)
    weight = dot(order, weight_ref[...]).astype(jnp.bfloat16)
    x = dot(feats_ref[...], weight).astype(jnp.bfloat16).astype(jnp.float32)
    scale = lax.rsqrt(jnp.mean(x * x, axis=1, keepdims=True) + 1e-06)
    normed_x = (x * scale * gain_ref[...]).astype(jnp.bfloat16)
    factor = 1.0 / math.sqrt(HDIM)
    cosine = cos_ref[...]
    sine = sin_ref[...]
    qk = dot(normed_x, qkv_ref[:, : 2 * INNER])
    for block in range(INNER // 128):
        cols = slice(block * 128, (block + 1) * 128)
        q = qk[:, cols]
        k = qk[:, INNER + block * 128 : INNER + (block + 1) * 128]
        query_s[:, cols] = ((q * cosine + swap_halves(q) * sine) * factor).astype(jnp.bfloat16)
        key_s[:, cols] = (k * cosine + swap_halves(k) * sine).astype(jnp.bfloat16)
    value_b = dot(normed_x, qkv_ref[:, 2 * INNER :]).astype(jnp.bfloat16)
    grad_mixed = dot(grads_ref[...], outw_ref[...], ((1,), (1,))).astype(jnp.bfloat16)
    for pair in range(HEADS // 2):
        cols = slice(pair * 128, (pair + 1) * 128)
        results = []
        for side in range(2):
            head = slice(side * HDIM, (side + 1) * HDIM)
            head_q = query_s[:, cols][:, head]
            head_k = key_s[:, cols][:, head]
            head_v = value_b[:, cols][:, head]
            head_g = grad_mixed[:, cols][:, head]
            scores = dot(head_q, head_k, ((1,), (1,)))
            peak = jnp.max(scores, axis=1, keepdims=True)
            expo = jnp.exp(scores - peak)
            probs = expo / jnp.sum(expo, axis=1, keepdims=True)
            probs_b = probs.astype(jnp.bfloat16)
            mixed = dot(probs_b, head_v)
            grad_p = dot(head_g, head_v, ((1,), (1,)))
            grad_v = dot(probs_b, head_g, ((0,), (0,)))
            row_dot = jnp.sum(probs * grad_p, axis=1, keepdims=True)
            grad_s = (probs * (grad_p - row_dot)).astype(jnp.bfloat16)
            grad_q = dot(grad_s, head_k)
            grad_k = dot(grad_s, head_q, ((0,), (0,)))
            results.append((mixed, grad_q, grad_k, grad_v))
        mixed, grad_q, grad_k, grad_v = (
            jnp.concatenate([low, high], axis=1) for low, high in zip(*results)
        )
        mixed_s[:, cols] = mixed.astype(jnp.bfloat16)
        grad_q = grad_q * factor
        gproj_s[:, cols] = (grad_q * cosine - swap_halves(grad_q) * sine).astype(jnp.bfloat16)
        gproj_s[:, INNER + pair * 128 : INNER + (pair + 1) * 128] = (
            grad_k * cosine - swap_halves(grad_k) * sine
        ).astype(jnp.bfloat16)
        gproj_s[:, 2 * INNER + pair * 128 : 2 * INNER + (pair + 1) * 128] = grad_v.astype(
            jnp.bfloat16
        )
    mixed_b = mixed_s[...]
    attended_ref[...] = (x + dot(mixed_b, outw_ref[...])).astype(jnp.bfloat16)
    for block in range(3 * INNER // D):
        part = dot(normed_x, gproj_s[:, block * D : (block + 1) * D], ((0,), (0,)))
        partial_ref[block * D : (block + 1) * D, :] = (part * factor_all).astype(jnp.bfloat16)
    part = dot(mixed_b, grads_ref[...], ((0,), (0,)))
    partial_ref[3 * INNER :, :] = (part * factor_all).astype(jnp.bfloat16)


def unpack_kernel(gathered_ref, grad_qkv_ref, grad_out_ref):
    for block in range(3 * INNER // D):
        grad_qkv_ref[:, block * D : (block + 1) * D] = gathered_ref[
            block * D : (block + 1) * D, :
        ].astype(jnp.float32)
    grad_out_ref[...] = gathered_ref[3 * INNER :, :].astype(jnp.float32)


def whole(memory_space=pltpu.VMEM):
    return pl.BlockSpec(memory_space=memory_space)


def spectrum(frames_here, widths_own, starts_own, audio, rim, gain, place):
    rows, own = audio.shape
    total = rows * frames_here
    own_bands = place.shape[1] // MAXW
    return pl.pallas_call(
        lambda *refs: spectrum_kernel(frames_here, *refs),
        out_shape=jax.ShapeDtypeStruct((own_bands * total // 2, FEAT), jnp.bfloat16),
        in_specs=[whole(pltpu.SMEM)] * 2 + [whole()] * 7,
        out_specs=whole(),
        scratch_shapes=[
            pltpu.VMEM((rows, WIN), jnp.float32),
            pltpu.VMEM((rows, WIN), jnp.float32),
            pltpu.VMEM((WIN // 128, total, 128), jnp.float32),
            pltpu.VMEM((OUTER * total, 2 * SPAN), jnp.float32),
            pltpu.VMEM((6 * total, BINS), jnp.bfloat16),
            pltpu.VMEM((BINS, own_bands * MAXW), jnp.bfloat16),
        ],
        name="spectrum",
    )(
        widths_own,
        starts_own,
        audio,
        rim,
        gain,
        place,
        jnp.asarray(window_table()),
        jnp.asarray(twiddle_table()),
        jnp.asarray(inner_table()),
    )


def layer(feats, weight, grads, norm_gain, qkv_weight, out_weight, factor_all):
    cosine, sine = rotary_table(np.arange(FRAMES))
    return pl.pallas_call(
        lambda *refs: layer_kernel(*refs, factor_all=factor_all),
        out_shape=(
            jax.ShapeDtypeStruct((FRAMES, D), jnp.bfloat16),
            jax.ShapeDtypeStruct((4 * INNER, D), jnp.bfloat16),
        ),
        in_specs=[whole()] * 8,
        out_specs=(whole(),) * 2,
        scratch_shapes=[
            pltpu.VMEM((FRAMES, INNER), jnp.bfloat16),
            pltpu.VMEM((FRAMES, INNER), jnp.bfloat16),
            pltpu.VMEM((FRAMES, INNER), jnp.bfloat16),
            pltpu.VMEM((FRAMES, 3 * INNER), jnp.bfloat16),
        ],
        name="layer",
    )(
        feats,
        weight,
        grads,
        norm_gain.reshape(1, D),
        qkv_weight,
        out_weight,
        jnp.asarray(cosine),
        jnp.asarray(sine),
    )


def unpack(gathered):
    return pl.pallas_call(
        unpack_kernel,
        out_shape=(
            jax.ShapeDtypeStruct((D, 3 * INNER), jnp.float32),
            jax.ShapeDtypeStruct((INNER, D), jnp.float32),
        ),
        in_specs=[whole()],
        out_specs=(whole(),) * 2,
        name="unpack",
    )(gathered)


def exchange(blocks, axis):
    return lax.all_to_all(blocks, axis, split_axis=0, concat_axis=0, tiled=True)


def reduced(blocks):
    return jnp.sum(blocks.astype(jnp.float32), axis=0).astype(jnp.bfloat16)


def scatter_sum(values, axis):
    count = lax.axis_size(axis)
    blocks = values.reshape(count, values.shape[0] // count, values.shape[1])
    return reduced(exchange(blocks, axis))


def gather(values, axis):
    count = lax.axis_size(axis)
    blocks = jnp.broadcast_to(values[None], (count,) + values.shape)
    return exchange(blocks, axis).reshape(count * values.shape[0], values.shape[1])


def body(
    audio_clips, band_widths, band_gain, band_weight, norm_gain, qkv_weight, out_weight, cotangent
):
    tm = lax.axis_size("tm")
    band_at = lax.axis_index("x") * lax.axis_size("core") + lax.axis_index("core")
    own_bands = band_gain.shape[0]
    frame_block = audio_clips.shape[2] // HOP
    audio = jnp.transpose(audio_clips, (1, 0, 2)).reshape(2 * CLIPS, -1)
    rim = lax.ppermute(
        audio[:, : WIN - HOP], "tm", [(source, source - 1) for source in range(1, tm)]
    )
    sequences = own_bands * CLIPS
    rows = FEAT // tm
    early = jnp.concatenate(
        [
            cotangent.reshape(sequences, frame_block, D),
            jnp.broadcast_to(band_weight[:, None], (own_bands, CLIPS, rows, D)).reshape(
                sequences, rows, D
            ),
        ],
        axis=1,
    )
    early = exchange(early, "tm")
    grads = early[:, :frame_block].reshape(FRAMES, D)
    weight = early[:, frame_block:].reshape(FEAT, D)
    starts = jnp.cumsum(band_widths, dtype=jnp.int32) - band_widths
    first_band = band_at * own_bands
    widths_own = lax.dynamic_slice_in_dim(band_widths, first_band, own_bands)
    starts_own = lax.dynamic_slice_in_dim(starts, first_band, own_bands)
    within = lax.iota(jnp.int32, MAXW)[None, :]
    place = jnp.where(within < widths_own[:, None], starts_own[:, None] + within, -1)
    gain = jnp.transpose(band_gain.reshape(own_bands, MAXW, 4), (0, 2, 1))
    normed = spectrum(
        frame_block,
        widths_own.reshape(1, own_bands),
        starts_own.reshape(1, own_bands),
        audio,
        rim,
        gain,
        place.reshape(1, own_bands * MAXW),
    )
    feats = exchange(normed.reshape(sequences, frame_block, FEAT), "tm").reshape(FRAMES, FEAT)
    factor_all = 1.0 / math.sqrt(BANDS * CLIPS * FRAMES)
    attended, partial = layer(
        feats, weight, grads, norm_gain, qkv_weight, out_weight, factor_all
    )
    partial = scatter_sum(scatter_sum(partial, "core"), "x")
    both = jnp.concatenate(
        [attended.reshape(tm, frame_block, D), partial.reshape(tm, -1, D)], axis=1
    )
    both = exchange(both, "tm")
    attended_out = both[:, :frame_block].reshape(own_bands, CLIPS, frame_block, D)
    total = reduced(both[:, frame_block:])
    for axis in ("tm", "x", "core"):
        total = gather(total, axis)
    grad_qkv, grad_out = unpack(total)
    return (attended_out, grad_qkv, grad_out)


def solution(mesh):
    split = Mesh(mesh.devices.reshape(mesh.shape["tm"], -1, 2), ("tm", "x", "core"))
    band = ("x", "core")
    return jax.shard_map(
        body,
        mesh=split,
        in_specs=(
            P(None, None, "tm"),
            P(),
            P(band, None),
            P(band, "tm", None),
            P(),
            P(),
            P(),
            P(band, None, "tm", None),
        ),
        out_specs=(P(band, None, "tm", None), P(), P()),
        check_vma=False,
    )
```

```python
import math

import jax
import jax.numpy as jnp
import numpy as np
from jax import lax
from jax.experimental import pallas as pl
from jax.experimental.pallas import tpu as pltpu
from jax.sharding import Mesh, PartitionSpec as P


D = 384
HEADS = 8
HDIM = 64
WIN = 2048
HOP = 441
BANDS = 64
MAXW = 128
CLIPS = 8
INNER = 512
BINS = 1024
FEAT = 512
FRAMES = 256
TIME = ("z", "y")
BAND = ("x", "core")

OUTER = 8
SPAN = WIN // OUTER
HIGH = BINS // OUTER


def window_table():
    sample_at = np.arange(WIN, dtype=np.float64)
    taper = (0.5 - 0.5 * np.cos(sample_at * (2.0 * np.pi / WIN))) / np.sqrt(WIN)
    return taper.reshape(1, WIN).astype(np.float32)


def twiddle_table():
    phase = np.outer(np.arange(OUTER), np.arange(SPAN)) % WIN
    angle = phase * (2.0 * np.pi / WIN)
    return np.concatenate([np.cos(angle), np.sin(angle)], axis=0).astype(np.float32)


def inner_table():
    phase = np.outer(np.arange(SPAN), np.arange(HIGH)) % SPAN
    angle = phase * (2.0 * np.pi / SPAN)
    real, imag = np.cos(angle), np.sin(angle)
    return np.concatenate(
        [np.concatenate([real, -imag], axis=1), np.concatenate([imag, real], axis=1)], axis=0
    ).astype(np.float32)


def rotary_table(frame_order):
    freq = np.exp(np.arange(HDIM // 2, dtype=np.float32) * np.float32(-2.0 * math.log(10000.0) / HDIM))
    angle = (frame_order.astype(np.float32)[:, None] * freq.astype(np.float32)[None, :]).astype(np.float64)
    cosine, sine = np.cos(angle), np.sin(angle)
    return (
        np.concatenate([cosine] * 4, axis=1).astype(np.float32),
        np.concatenate([-sine, sine, -sine, sine], axis=1).astype(np.float32),
    )


def split_bf16(values):
    parts = []
    for _ in range(3):
        kept = values.astype(jnp.bfloat16)
        parts.append(kept)
        values = values - kept.astype(jnp.float32)
    return parts


def one_hot(hit):
    return jnp.where(hit, 1.0, 0.0).astype(jnp.bfloat16)


def spectrum_kernel(
    place_ref,
    widths_ref,
    audio_ref,
    rim_ref,
    gain_ref,
    taper_ref,
    twiddle_ref,
    inner_ref,
    out_ref,
    lead,
    tail,
    framed,
    stage,
    bins,
    pick,
):
    own = audio_ref.shape[2]
    rows = audio_ref.shape[0] * audio_ref.shape[1]
    frames_here = own // HOP
    total = rows * frames_here
    own_bands = gain_ref.shape[0]
    for c in range(CLIPS):
        lead[2 * c : 2 * c + 2, :own] = audio_ref[c]
        tail[2 * c : 2 * c + 2, :own] = rim_ref[c]
    lane = lax.broadcasted_iota(jnp.int32, (rows, WIN), 1)
    for f in range(frames_here):
        here = own - HOP * f
        head = lead[...] if f == 0 else pltpu.roll(lead[...], WIN - HOP * f, 1)
        rest = pltpu.roll(tail[...], here % WIN, 1)
        frame = jnp.where(lane < here, head, rest) * taper_ref[...]
        for block in range(WIN // 128):
            framed[block, pl.ds(f, rows, stride=frames_here), :] = frame[
                :, block * 128 : (block + 1) * 128
            ]
    root = math.sqrt(0.5)
    for half in range(SPAN // 128):
        x = [framed[2 * n + half] for n in range(OUTER)]
        e0, e1, e2, e3 = x[0] + x[4], x[1] + x[5], x[2] + x[6], x[3] + x[7]
        d0, d1, d2, d3 = x[0] - x[4], x[1] - x[5], x[2] - x[6], x[3] - x[7]
        s02, s13 = e0 + e2, e1 + e3
        p = (d1 - d3) * root
        q = (d1 + d3) * root
        real = [s02 + s13, d0 + p, e0 - e2, d0 - p, s02 - s13]
        imag = [None, -(q + d2), e3 - e1, d2 - q, None]
        lanes = slice(half * 128, (half + 1) * 128)
        for low in range(OUTER):
            if low <= 4:
                re, im = real[low], imag[low]
            else:
                re, im = real[8 - low], -imag[8 - low]
            at = slice(low * total, (low + 1) * total)
            if low == 0:
                stage[at, half * 128 : (half + 1) * 128] = re
                stage[at, SPAN + half * 128 : SPAN + (half + 1) * 128] = jnp.zeros_like(re)
                continue
            c = twiddle_ref[low : low + 1, lanes]
            s = twiddle_ref[OUTER + low : OUTER + low + 1, lanes]
            if im is None:
                zr, zi = re * c, -(re * s)
            else:
                zr, zi = re * c + im * s, im * c - re * s
            stage[at, half * 128 : (half + 1) * 128] = zr
            stage[at, SPAN + half * 128 : SPAN + (half + 1) * 128] = zi
    made = jnp.dot(
        stage[...],
        inner_ref[...],
        preferred_element_type=jnp.float32,
        precision=lax.Precision.HIGHEST,
    )
    for low in range(OUTER):
        cols = slice(low * HIGH, (low + 1) * HIGH)
        for part in range(2):
            piece = made[low * total : (low + 1) * total, part * HIGH : (part + 1) * HIGH]
            for split, kept in enumerate(split_bf16(piece)):
                at = (split * 2 + part) * total
                bins[at : at + total, cols] = kept
    first_band = place_ref[0] * own_bands
    start = lax.fori_loop(0, first_band, lambda i, past: past + widths_ref[i], jnp.int32(0))
    within = lax.broadcasted_iota(jnp.int32, (1, MAXW), 1)
    high_at = OUTER * lax.broadcasted_iota(jnp.int32, (HIGH, MAXW), 0)
    counts = []
    for band in range(own_bands):
        width = widths_ref[first_band + band]
        target = jnp.where(within < width, start + within, -1)
        for low in range(OUTER):
            pick[low * HIGH : (low + 1) * HIGH, band * MAXW : (band + 1) * MAXW] = one_hot(
                high_at == target - low
            )
        counts.append((4 * width).astype(jnp.float32))
        start = start + width
    chosen = jnp.dot(bins[...], pick[...], preferred_element_type=jnp.float32)
    exact = chosen[: 2 * total] + chosen[2 * total : 4 * total] + chosen[4 * total :]
    feature = lax.broadcasted_iota(jnp.int32, (FEAT, FEAT), 0)
    column = lax.broadcasted_iota(jnp.int32, (FEAT, FEAT), 1)
    order = one_hot(feature == (column % MAXW) * 4 + column // MAXW)
    gain = sum(
        jnp.dot(part, order, preferred_element_type=jnp.float32)
        for part in split_bf16(gain_ref[...])
    )
    row = lax.broadcasted_iota(jnp.int32, (total, 1), 0)
    for band in range(own_bands):
        cols = slice(band * MAXW, (band + 1) * MAXW)
        re = exact[:total, cols]
        im = exact[total:, cols]
        power = jnp.sum(re * re + im * im, axis=1, keepdims=True)
        ahead = pltpu.roll(power, total - frames_here, 0)
        behind = pltpu.roll(power, frames_here, 0)
        power = power + jnp.where(row % (2 * frames_here) < frames_here, ahead, behind)
        inverse = lax.rsqrt(jnp.maximum(power / counts[band], 0.25))
        for r in range(2):
            value = ((re, im)[r] * inverse).reshape(CLIPS, 2 * frames_here, MAXW)
            for a in range(2):
                which = 2 * a + r
                lanes = slice(which * MAXW, (which + 1) * MAXW)
                own_gain = gain[band : band + 1, lanes]
                out_ref[band * CLIPS : (band + 1) * CLIPS, :, lanes] = (
                    value[:, a * frames_here : (a + 1) * frames_here, :] * own_gain[None]
                ).astype(jnp.bfloat16)


def swap_halves(values):
    width = values.shape[1]
    lane = lax.broadcasted_iota(jnp.int32, values.shape, 1)
    forward = pltpu.roll(values, width - HDIM // 2, 1)
    backward = pltpu.roll(values, HDIM // 2, 1)
    return jnp.where(lane % HDIM < HDIM // 2, forward, backward)


def dot(left, right, dims=((1,), (0,))):
    return lax.dot_general(left, right, (dims, ((), ())), preferred_element_type=jnp.float32)


def layer_kernel(
    feats_ref,
    weight_ref,
    grads_ref,
    gain_ref,
    qkv_ref,
    outw_ref,
    cos_ref,
    sin_ref,
    core_ref,
    attended_ref,
    keep_ref,
    send_ref,
    query_s,
    key_s,
    mixed_s,
    gproj_s,
    halves,
    *,
    factor_all,
):
    natural = lax.broadcasted_iota(jnp.int32, (FEAT, FEAT), 1)
    wanted = lax.broadcasted_iota(jnp.int32, (FEAT, FEAT), 0)
    wanted = (wanted % MAXW) * 4 + wanted // MAXW
    order = jnp.where(natural == wanted, 1.0, 0.0).astype(jnp.bfloat16)
    weight = dot(order, weight_ref[...]).astype(jnp.bfloat16)
    x = dot(feats_ref[...], weight).astype(jnp.bfloat16).astype(jnp.float32)
    scale = lax.rsqrt(jnp.mean(x * x, axis=1, keepdims=True) + 1e-06)
    normed_x = (x * scale * gain_ref[...]).astype(jnp.bfloat16)
    factor = 1.0 / math.sqrt(HDIM)
    cosine = cos_ref[...]
    sine = sin_ref[...]
    qk = dot(normed_x, qkv_ref[:, : 2 * INNER])
    for block in range(INNER // 128):
        cols = slice(block * 128, (block + 1) * 128)
        q = qk[:, cols]
        k = qk[:, INNER + block * 128 : INNER + (block + 1) * 128]
        query_s[:, cols] = ((q * cosine + swap_halves(q) * sine) * factor).astype(jnp.bfloat16)
        key_s[:, cols] = (k * cosine + swap_halves(k) * sine).astype(jnp.bfloat16)
    value_b = dot(normed_x, qkv_ref[:, 2 * INNER :]).astype(jnp.bfloat16)
    grad_mixed = dot(grads_ref[...], outw_ref[...], ((1,), (1,))).astype(jnp.bfloat16)
    for pair in range(HEADS // 2):
        cols = slice(pair * 128, (pair + 1) * 128)
        results = []
        for side in range(2):
            head = slice(side * HDIM, (side + 1) * HDIM)
            head_q = query_s[:, cols][:, head]
            head_k = key_s[:, cols][:, head]
            head_v = value_b[:, cols][:, head]
            head_g = grad_mixed[:, cols][:, head]
            scores = dot(head_q, head_k, ((1,), (1,)))
            peak = jnp.max(scores, axis=1, keepdims=True)
            expo = jnp.exp(scores - peak)
            probs = expo / jnp.sum(expo, axis=1, keepdims=True)
            probs_b = probs.astype(jnp.bfloat16)
            mixed = dot(probs_b, head_v)
            grad_p = dot(head_g, head_v, ((1,), (1,)))
            grad_v = dot(probs_b, head_g, ((0,), (0,)))
            row_dot = jnp.sum(probs * grad_p, axis=1, keepdims=True)
            grad_s = (probs * (grad_p - row_dot)).astype(jnp.bfloat16)
            grad_q = dot(grad_s, head_k)
            grad_k = dot(grad_s, head_q, ((0,), (0,)))
            results.append((mixed, grad_q, grad_k, grad_v))
        mixed, grad_q, grad_k, grad_v = (
            jnp.concatenate([low, high], axis=1) for low, high in zip(*results)
        )
        mixed_s[:, cols] = mixed.astype(jnp.bfloat16)
        grad_q = grad_q * factor
        gproj_s[:, cols] = (grad_q * cosine - swap_halves(grad_q) * sine).astype(jnp.bfloat16)
        gproj_s[:, INNER + pair * 128 : INNER + (pair + 1) * 128] = (
            grad_k * cosine - swap_halves(grad_k) * sine
        ).astype(jnp.bfloat16)
        gproj_s[:, 2 * INNER + pair * 128 : 2 * INNER + (pair + 1) * 128] = grad_v.astype(
            jnp.bfloat16
        )
    mixed_b = mixed_s[...]
    attended_ref[...] = (x + dot(mixed_b, outw_ref[...])).astype(jnp.bfloat16)
    core = core_ref[0]
    half_rows = 2 * INNER

    def place(first, values):
        values = (values * factor_all).astype(jnp.bfloat16)
        at = first
        while at < first + D:
            half, row = divmod(at, half_rows)
            end = min(first + D, (half + 1) * half_rows)
            slot = core if half == 0 else 1 - core
            halves[slot, row : row + end - at, :] = values[at - first : end - first]
            at = end

    for block in range(3 * INNER // D):
        place(block * D, dot(normed_x, gproj_s[:, block * D : (block + 1) * D], ((0,), (0,))))
    part = dot(mixed_b, grads_ref[...], ((0,), (0,))) * factor_all
    halves[1 - core, half_rows - INNER :, :] = part.astype(jnp.bfloat16)
    keep_ref[...] = halves[0]
    send_ref[...] = halves[1]


def unpack_kernel(core_ref, own_ref, other_ref, grad_qkv_ref, grad_out_ref):
    half_rows = own_ref.shape[0]
    first = core_ref[0] == 0

    def rows(start, stop):
        half = start // half_rows
        at = slice(start - half * half_rows, stop - half * half_rows)
        own, other = own_ref[at, :], other_ref[at, :]
        return lax.select(first, *((own, other) if half == 0 else (other, own))).astype(jnp.float32)

    for block in range(3 * INNER // D):
        at = block * D
        while at < (block + 1) * D:
            end = min((block + 1) * D, (at // half_rows + 1) * half_rows)
            grad_qkv_ref[at - block * D : end - block * D, block * D : (block + 1) * D] = rows(at, end)
            at = end
    grad_out_ref[...] = rows(3 * INNER, 4 * INNER)


def whole(memory_space=pltpu.VMEM):
    return pl.BlockSpec(memory_space=memory_space)


def spectrum(band_at, band_widths, audio, rim, gain):
    rows, own = audio.shape[0] * audio.shape[1], audio.shape[2]
    frames_here = own // HOP
    total = rows * frames_here
    own_bands = gain.shape[0]
    return pl.pallas_call(
        spectrum_kernel,
        out_shape=jax.ShapeDtypeStruct((own_bands * CLIPS, frames_here, FEAT), jnp.bfloat16),
        in_specs=[whole(pltpu.SMEM)] * 2 + [whole()] * 6,
        out_specs=whole(),
        scratch_shapes=[
            pltpu.VMEM((rows, WIN), jnp.float32),
            pltpu.VMEM((rows, WIN), jnp.float32),
            pltpu.VMEM((WIN // 128, total, 128), jnp.float32),
            pltpu.VMEM((OUTER * total, 2 * SPAN), jnp.float32),
            pltpu.VMEM((6 * total, BINS), jnp.bfloat16),
            pltpu.VMEM((BINS, own_bands * MAXW), jnp.bfloat16),
        ],
        name="spectrum",
    )(
        band_at.reshape(1),
        band_widths,
        audio,
        rim,
        gain,
        jnp.asarray(window_table()),
        jnp.asarray(twiddle_table()),
        jnp.asarray(inner_table()),
    )


def layer(feats, weight, grads, norm_gain, qkv_weight, out_weight, core, factor_all):
    cosine, sine = rotary_table(np.arange(FRAMES))
    return pl.pallas_call(
        lambda *refs: layer_kernel(*refs, factor_all=factor_all),
        out_shape=(
            jax.ShapeDtypeStruct((FRAMES, D), jnp.bfloat16),
            jax.ShapeDtypeStruct((2 * INNER, D), jnp.bfloat16),
            jax.ShapeDtypeStruct((2 * INNER, D), jnp.bfloat16),
        ),
        in_specs=[whole()] * 8 + [whole(pltpu.SMEM)],
        out_specs=(whole(),) * 3,
        scratch_shapes=[
            pltpu.VMEM((FRAMES, INNER), jnp.bfloat16),
            pltpu.VMEM((FRAMES, INNER), jnp.bfloat16),
            pltpu.VMEM((FRAMES, INNER), jnp.bfloat16),
            pltpu.VMEM((FRAMES, 3 * INNER), jnp.bfloat16),
            pltpu.VMEM((2, 2 * INNER, D), jnp.bfloat16),
        ],
        name="layer",
    )(
        feats,
        weight,
        grads,
        norm_gain.reshape(1, D),
        qkv_weight,
        out_weight,
        jnp.asarray(cosine),
        jnp.asarray(sine),
        core,
    )


def unpack(core, own, other):
    return pl.pallas_call(
        unpack_kernel,
        out_shape=(
            jax.ShapeDtypeStruct((D, 3 * INNER), jnp.float32),
            jax.ShapeDtypeStruct((INNER, D), jnp.float32),
        ),
        in_specs=[whole(pltpu.SMEM), whole(), whole()],
        out_specs=(whole(),) * 2,
        name="unpack",
    )(core, own, other)


def exchange(blocks, axis):
    return lax.all_to_all(blocks, axis, split_axis=0, concat_axis=0, tiled=True)


def reduced(blocks):
    return jnp.sum(blocks.astype(jnp.float32), axis=0).astype(jnp.bfloat16)


def scatter_sum(values, axis):
    count = lax.axis_size(axis)
    blocks = values.reshape(count, values.shape[0] // count, values.shape[1])
    return reduced(exchange(blocks, axis))


def gather(values, axis):
    count = lax.axis_size(axis)
    blocks = jnp.broadcast_to(values[None], (count,) + values.shape)
    return exchange(blocks, axis).reshape(count * values.shape[0], values.shape[1])


def staged(
    audio_clips, band_widths, band_gain, band_weight, norm_gain, qkv_weight, out_weight, cotangent
):
    tm = lax.axis_size(TIME)
    band_at = lax.axis_index("x") * lax.axis_size("core") + lax.axis_index("core")
    own_bands = band_gain.shape[0]
    frame_block = audio_clips.shape[2] // HOP
    rim = lax.ppermute(audio_clips, TIME, [(source, source - 1) for source in range(1, tm)])
    sequences = own_bands * CLIPS
    rows = FEAT // tm
    early = jnp.concatenate(
        [
            cotangent.reshape(sequences, frame_block, D),
            jnp.broadcast_to(band_weight[:, None], (own_bands, CLIPS, rows, D)).reshape(
                sequences, rows, D
            ),
        ],
        axis=1,
    )
    early = exchange(early, TIME)
    grads = early[:, :frame_block].reshape(FRAMES, D)
    weight = early[:, frame_block:].reshape(FEAT, D)
    normed = spectrum(band_at, band_widths, audio_clips, rim, band_gain)
    feats = exchange(normed, TIME).reshape(FRAMES, FEAT)
    factor_all = 1.0 / math.sqrt(BANDS * CLIPS * FRAMES)
    core = lax.axis_index("core").reshape(1)
    attended, keep, send = layer(
        feats, weight, grads, norm_gain, qkv_weight, out_weight, core, factor_all
    )
    swap = [(0, 1), (1, 0)]
    partial = keep.astype(jnp.float32) + lax.ppermute(send, "core", swap).astype(jnp.float32)
    partial = scatter_sum(partial.astype(jnp.bfloat16), "x")
    both = jnp.concatenate(
        [attended.reshape(tm, frame_block, D), partial.reshape(tm, -1, D)], axis=1
    )
    both = exchange(both, TIME)
    attended_out = both[:, :frame_block].reshape(own_bands, CLIPS, frame_block, D)
    partial = gather(gather(reduced(both[:, frame_block:]), TIME), "x")
    grad_qkv, grad_out = unpack(core, partial, lax.ppermute(partial, "core", swap))
    return (attended_out, grad_qkv, grad_out)


def solution(mesh):
    split = Mesh(mesh.devices.reshape(8, -1, 4, 2), TIME + BAND)
    return jax.shard_map(
        staged,
        mesh=split,
        in_specs=(
            P(None, None, TIME),
            P(),
            P(BAND, None),
            P(BAND, TIME, None),
            P(),
            P(),
            P(),
            P(BAND, None, TIME, None),
        ),
        out_specs=(P(BAND, None, TIME, None), P(), P()),
        check_vma=False,
    )
```

```python
import math

import jax
import jax.numpy as jnp
import numpy as np
from jax import lax
from jax.experimental import pallas as pl
from jax.experimental.pallas import tpu as pltpu
from jax.sharding import Mesh, PartitionSpec as P


D = 384
HEADS = 8
HDIM = 64
WIN = 2048
HOP = 441
BANDS = 64
MAXW = 128
CLIPS = 8
INNER = 512
BINS = 1024
FEAT = 512
FRAMES = 256
TIME = ("z", "y")
BAND = ("x", "core")

OUTER = 8
SPAN = WIN // OUTER
HIGH = BINS // OUTER


def window_table():
    sample_at = np.arange(WIN, dtype=np.float64)
    taper = (0.5 - 0.5 * np.cos(sample_at * (2.0 * np.pi / WIN))) / np.sqrt(WIN)
    return taper.reshape(1, WIN).astype(np.float32)


def twiddle_table():
    phase = np.outer(np.arange(OUTER), np.arange(SPAN)) % WIN
    angle = phase * (2.0 * np.pi / WIN)
    return np.concatenate([np.cos(angle), np.sin(angle)], axis=0).astype(np.float32)


def inner_table():
    phase = np.outer(np.arange(SPAN), np.arange(HIGH)) % SPAN
    angle = phase * (2.0 * np.pi / SPAN)
    real, imag = np.cos(angle), np.sin(angle)
    return np.concatenate(
        [np.concatenate([real, -imag], axis=1), np.concatenate([imag, real], axis=1)], axis=0
    ).astype(np.float32)


def rotary_table(frame_order):
    freq = np.exp(np.arange(HDIM // 2, dtype=np.float32) * np.float32(-2.0 * math.log(10000.0) / HDIM))
    angle = (frame_order.astype(np.float32)[:, None] * freq.astype(np.float32)[None, :]).astype(np.float64)
    cosine, sine = np.cos(angle), np.sin(angle)
    return (
        np.concatenate([cosine] * 4, axis=1).astype(np.float32),
        np.concatenate([-sine, sine, -sine, sine], axis=1).astype(np.float32),
    )


def split_bf16(values):
    parts = []
    for _ in range(3):
        kept = values.astype(jnp.bfloat16)
        parts.append(kept)
        values = values - kept.astype(jnp.float32)
    return parts


def one_hot(hit):
    return jnp.where(hit, 1.0, 0.0).astype(jnp.bfloat16)


def spectrum_kernel(
    place_ref,
    widths_ref,
    audio_ref,
    rim_ref,
    gain_ref,
    taper_ref,
    twiddle_ref,
    inner_ref,
    out_ref,
    lead,
    tail,
    framed,
    stage,
    bins,
    pick,
):
    own = audio_ref.shape[2]
    rows = audio_ref.shape[0] * audio_ref.shape[1]
    frames_here = own // HOP
    total = rows * frames_here
    own_bands = gain_ref.shape[0]
    for c in range(CLIPS):
        lead[2 * c : 2 * c + 2, :own] = audio_ref[c]
        tail[2 * c : 2 * c + 2, :own] = rim_ref[c]
    lane = lax.broadcasted_iota(jnp.int32, (rows, WIN), 1)
    for f in range(frames_here):
        here = own - HOP * f
        head = lead[...] if f == 0 else pltpu.roll(lead[...], WIN - HOP * f, 1)
        rest = pltpu.roll(tail[...], here % WIN, 1)
        frame = jnp.where(lane < here, head, rest) * taper_ref[...]
        for block in range(WIN // 128):
            framed[block, pl.ds(f, rows, stride=frames_here), :] = frame[
                :, block * 128 : (block + 1) * 128
            ]
    root = math.sqrt(0.5)
    for half in range(SPAN // 128):
        x = [framed[2 * n + half] for n in range(OUTER)]
        e0, e1, e2, e3 = x[0] + x[4], x[1] + x[5], x[2] + x[6], x[3] + x[7]
        d0, d1, d2, d3 = x[0] - x[4], x[1] - x[5], x[2] - x[6], x[3] - x[7]
        s02, s13 = e0 + e2, e1 + e3
        p = (d1 - d3) * root
        q = (d1 + d3) * root
        real = [s02 + s13, d0 + p, e0 - e2, d0 - p, s02 - s13]
        imag = [None, -(q + d2), e3 - e1, d2 - q, None]
        lanes = slice(half * 128, (half + 1) * 128)
        for low in range(OUTER):
            if low <= 4:
                re, im = real[low], imag[low]
            else:
                re, im = real[8 - low], -imag[8 - low]
            at = slice(low * total, (low + 1) * total)
            if low == 0:
                stage[at, half * 128 : (half + 1) * 128] = re
                stage[at, SPAN + half * 128 : SPAN + (half + 1) * 128] = jnp.zeros_like(re)
                continue
            c = twiddle_ref[low : low + 1, lanes]
            s = twiddle_ref[OUTER + low : OUTER + low + 1, lanes]
            if im is None:
                zr, zi = re * c, -(re * s)
            else:
                zr, zi = re * c + im * s, im * c - re * s
            stage[at, half * 128 : (half + 1) * 128] = zr
            stage[at, SPAN + half * 128 : SPAN + (half + 1) * 128] = zi
    made = jnp.dot(
        stage[...],
        inner_ref[...],
        preferred_element_type=jnp.float32,
        precision=lax.Precision.HIGHEST,
    )
    for low in range(OUTER):
        cols = slice(low * HIGH, (low + 1) * HIGH)
        for part in range(2):
            piece = made[low * total : (low + 1) * total, part * HIGH : (part + 1) * HIGH]
            for split, kept in enumerate(split_bf16(piece)):
                at = (split * 2 + part) * total
                bins[at : at + total, cols] = kept
    first_band = place_ref[0] * own_bands
    start = lax.fori_loop(0, first_band, lambda i, past: past + widths_ref[i], jnp.int32(0))
    within = lax.broadcasted_iota(jnp.int32, (1, MAXW), 1)
    high_at = OUTER * lax.broadcasted_iota(jnp.int32, (HIGH, MAXW), 0)
    counts = []
    for band in range(own_bands):
        width = widths_ref[first_band + band]
        target = jnp.where(within < width, start + within, -1)
        for low in range(OUTER):
            pick[low * HIGH : (low + 1) * HIGH, band * MAXW : (band + 1) * MAXW] = one_hot(
                high_at == target - low
            )
        counts.append((4 * width).astype(jnp.float32))
        start = start + width
    chosen = jnp.dot(bins[...], pick[...], preferred_element_type=jnp.float32)
    exact = chosen[: 2 * total] + chosen[2 * total : 4 * total] + chosen[4 * total :]
    feature = lax.broadcasted_iota(jnp.int32, (FEAT, FEAT), 0)
    column = lax.broadcasted_iota(jnp.int32, (FEAT, FEAT), 1)
    order = one_hot(feature == (column % MAXW) * 4 + column // MAXW)
    gain = sum(
        jnp.dot(part, order, preferred_element_type=jnp.float32)
        for part in split_bf16(gain_ref[...])
    )
    row = lax.broadcasted_iota(jnp.int32, (total, 1), 0)
    for band in range(own_bands):
        cols = slice(band * MAXW, (band + 1) * MAXW)
        re = exact[:total, cols]
        im = exact[total:, cols]
        power = jnp.sum(re * re + im * im, axis=1, keepdims=True)
        ahead = pltpu.roll(power, total - frames_here, 0)
        behind = pltpu.roll(power, frames_here, 0)
        power = power + jnp.where(row % (2 * frames_here) < frames_here, ahead, behind)
        inverse = lax.rsqrt(jnp.maximum(power / counts[band], 0.25))
        for r in range(2):
            value = ((re, im)[r] * inverse).reshape(CLIPS, 2 * frames_here, MAXW)
            for a in range(2):
                which = 2 * a + r
                lanes = slice(which * MAXW, (which + 1) * MAXW)
                own_gain = gain[band : band + 1, lanes]
                out_ref[band * CLIPS : (band + 1) * CLIPS, :, lanes] = (
                    value[:, a * frames_here : (a + 1) * frames_here, :] * own_gain[None]
                ).astype(jnp.bfloat16)


def dot(left, right, dims=((1,), (0,))):
    return lax.dot_general(left, right, (dims, ((), ())), preferred_element_type=jnp.float32)


def split_heads(values):
    low = lax.broadcasted_iota(jnp.int32, values.shape, 1) < HDIM
    return (
        jnp.where(low, values, 0.0).astype(jnp.bfloat16),
        jnp.where(low, 0.0, values).astype(jnp.bfloat16),
    )


def prepare_kernel(weight_ref, grads_ref, qkv_ref, outw_ref, embed_ref, heads_ref, swapped_ref):
    natural = lax.broadcasted_iota(jnp.int32, (FEAT, FEAT), 1)
    wanted = lax.broadcasted_iota(jnp.int32, (FEAT, FEAT), 0)
    order = one_hot(natural == (wanted % MAXW) * 4 + wanted // MAXW)
    embed_ref[...] = dot(order, weight_ref[...]).astype(jnp.bfloat16)
    grad_mixed = dot(grads_ref[...], outw_ref[...], ((1,), (1,)))
    for pair in range(HEADS // 2):
        low, high = split_heads(grad_mixed[:, pair * 128 : (pair + 1) * 128])
        heads_ref[pair, :FRAMES, :] = low
        heads_ref[pair, FRAMES:, :] = high
    row = lax.broadcasted_iota(jnp.int32, (128, 128), 0)
    lane = lax.broadcasted_iota(jnp.int32, (128, 128), 1)
    swap = one_hot(row == lane + jnp.where(lane % HDIM < HDIM // 2, HDIM // 2, -(HDIM // 2)))
    for block in range(2 * INNER // 128):
        cols = slice(block * 128, (block + 1) * 128)
        swapped_ref[:, cols] = dot(qkv_ref[:, cols], swap).astype(jnp.bfloat16)


def layer_kernel(
    core_ref,
    feats_ref,
    embed_ref,
    gain_ref,
    qkv_hbm,
    swapped_hbm,
    cos_hbm,
    sin_hbm,
    heads_hbm,
    outw_hbm,
    grads_hbm,
    attended_ref,
    keep_ref,
    send_ref,
    qkv_ref,
    swapped_ref,
    cos_ref,
    sin_ref,
    heads_ref,
    outw_ref,
    grads_ref,
    mixed_s,
    gproj_s,
    halves,
    sems,
    *,
    factor_all,
):
    pairs = (
        (qkv_hbm, qkv_ref),
        (swapped_hbm, swapped_ref),
        (cos_hbm, cos_ref),
        (sin_hbm, sin_ref),
        (heads_hbm, heads_ref),
        (outw_hbm, outw_ref),
        (grads_hbm, grads_ref),
    )
    copies = [
        pltpu.make_async_copy(source, target, sems.at[at])
        for at, (source, target) in enumerate(pairs)
    ]
    for copy in copies:
        copy.start()
    x = dot(feats_ref[...], embed_ref[...]).astype(jnp.bfloat16).astype(jnp.float32)
    scale = lax.rsqrt(jnp.mean(x * x, axis=1, keepdims=True) + 1e-06)
    normed_x = (x * scale * gain_ref[...]).astype(jnp.bfloat16)
    for copy in copies[:4]:
        copy.wait()
    factor = 1.0 / math.sqrt(HDIM)
    cosine = cos_ref[...]
    sine = sin_ref[...]
    for copy in copies[4:]:
        copy.wait()

    def opened(pair):
        cols = slice(pair * 128, (pair + 1) * 128)
        after = slice(INNER + pair * 128, INNER + (pair + 1) * 128)
        q, k, v = (
            dot(normed_x, qkv_ref[:, part * INNER + pair * 128 : part * INNER + (pair + 1) * 128])
            for part in range(3)
        )
        q_swap = dot(normed_x, swapped_ref[:, cols])
        k_swap = dot(normed_x, swapped_ref[:, after])
        query = split_heads((q * cosine + q_swap * sine) * factor)
        query_swap = split_heads((q_swap * cosine - q * sine) * factor)
        turned = k * cosine + k_swap * sine
        key = split_heads(turned)
        key_swap = split_heads(k_swap * cosine - k * sine)
        value = split_heads(v)
        stacked = jnp.concatenate(query, axis=0)
        scores = dot(stacked, turned.astype(jnp.bfloat16), ((1,), (1,)))
        grad_p = dot(heads_ref[pair], v.astype(jnp.bfloat16), ((1,), (1,)))
        both_q = jnp.concatenate([stacked, jnp.concatenate(query_swap, axis=0)], axis=1)
        both_k = [jnp.concatenate([a, b], axis=1) for a, b in zip(key, key_swap)]
        return scores, grad_p, both_q, both_k, value

    def closed(pair, scores, grad_p, both_q, both_k, value):
        cols = slice(pair * 128, (pair + 1) * 128)
        peak = jnp.max(scores, axis=1, keepdims=True)
        expo = jnp.exp(scores - peak)
        probs = expo / jnp.sum(expo, axis=1, keepdims=True)
        probs_b = probs.astype(jnp.bfloat16)
        row_dot = jnp.sum(probs * grad_p, axis=1, keepdims=True)
        grad_s = (probs * (grad_p - row_dot)).astype(jnp.bfloat16)
        mixed = dot(probs_b[:FRAMES], value[0]) + dot(probs_b[FRAMES:], value[1])
        grad_v = dot(probs_b, heads_ref[pair], ((0,), (0,)))
        grad_q = (dot(grad_s[:FRAMES], both_k[0]) + dot(grad_s[FRAMES:], both_k[1])) * factor
        grad_k = dot(grad_s, both_q, ((0,), (0,)))
        mixed_s[:, cols] = mixed.astype(jnp.bfloat16)
        for part, grad in enumerate((grad_q, grad_k)):
            turned = grad[:, :128] * cosine - grad[:, 128:] * sine
            gproj_s[:, part * INNER + pair * 128 : part * INNER + (pair + 1) * 128] = turned.astype(
                jnp.bfloat16
            )
        gproj_s[:, 2 * INNER + pair * 128 : 2 * INNER + (pair + 1) * 128] = grad_v.astype(
            jnp.bfloat16
        )

    ready = opened(0)
    for pair in range(HEADS // 2):
        following = opened(pair + 1) if pair + 1 < HEADS // 2 else None
        closed(pair, *ready)
        ready = following
    mixed_b = mixed_s[...]
    attended_ref[...] = (x + dot(mixed_b, outw_ref[...])).astype(jnp.bfloat16)
    core = core_ref[0]

    def place(first, values):
        values = (values * factor_all).astype(jnp.bfloat16)
        rows = values.shape[0] // 2
        halves[core, first : first + rows, :] = values[:rows]
        halves[1 - core, first : first + rows, :] = values[rows:]

    for block in range(3 * INNER // D):
        place(
            block * D // 2, dot(normed_x, gproj_s[:, block * D : (block + 1) * D], ((0,), (0,)))
        )
    place(3 * INNER // 2, dot(mixed_b, grads_ref[...], ((0,), (0,))))
    keep_ref[...] = halves[0]
    send_ref[...] = halves[1]


def unpack_kernel(core_ref, half_ref, *refs):
    grad_qkv_hbm, grad_out_hbm, wide, tall, sems = refs[-5:]
    rows = wide.shape[0]
    for block in range(3 * INNER // D):
        wide[:, block * D : (block + 1) * D] = half_ref[
            block * rows : (block + 1) * rows, :
        ].astype(jnp.float32)
    tall[...] = half_ref[3 * INNER // D * rows :, :].astype(jnp.float32)
    core = core_ref[0]
    copies = []
    for at, (source, target) in enumerate(((wide, grad_qkv_hbm), (tall, grad_out_hbm))):
        count = source.shape[0]
        place = target.at[pl.ds(pl.multiple_of(core * count, count), count), :]
        copies.append(pltpu.make_async_copy(source, place, sems.at[at]))
    for copy in copies:
        copy.start()
    for copy in copies:
        copy.wait()


def whole(memory_space=pltpu.VMEM):
    return pl.BlockSpec(memory_space=memory_space)


def spectrum(band_at, band_widths, audio, rim, gain):
    rows, own = audio.shape[0] * audio.shape[1], audio.shape[2]
    frames_here = own // HOP
    total = rows * frames_here
    own_bands = gain.shape[0]
    return pl.pallas_call(
        spectrum_kernel,
        out_shape=jax.ShapeDtypeStruct((own_bands * CLIPS, frames_here, FEAT), jnp.bfloat16),
        in_specs=[whole(pltpu.SMEM)] * 2 + [whole()] * 6,
        out_specs=whole(),
        scratch_shapes=[
            pltpu.VMEM((rows, WIN), jnp.float32),
            pltpu.VMEM((rows, WIN), jnp.float32),
            pltpu.VMEM((WIN // 128, total, 128), jnp.float32),
            pltpu.VMEM((OUTER * total, 2 * SPAN), jnp.float32),
            pltpu.VMEM((6 * total, BINS), jnp.bfloat16),
            pltpu.VMEM((BINS, own_bands * MAXW), jnp.bfloat16),
        ],
        name="spectrum",
    )(
        band_at.reshape(1),
        band_widths,
        audio,
        rim,
        gain,
        jnp.asarray(window_table()),
        jnp.asarray(twiddle_table()),
        jnp.asarray(inner_table()),
    )


def prepare(weight, grads, qkv_weight, out_weight):
    return pl.pallas_call(
        prepare_kernel,
        out_shape=(
            jax.ShapeDtypeStruct((FEAT, D), jnp.bfloat16),
            jax.ShapeDtypeStruct((HEADS // 2, 2 * FRAMES, 128), jnp.bfloat16),
            jax.ShapeDtypeStruct((D, 2 * INNER), jnp.bfloat16),
        ),
        in_specs=[whole()] * 4,
        out_specs=(whole(),) * 3,
        name="prepare",
    )(weight, grads, qkv_weight, out_weight)


def layer(core, feats, prepared, grads, norm_gain, qkv_weight, out_weight, factor_all):
    embed, heads, swapped = prepared
    cosine, sine = rotary_table(np.arange(FRAMES))
    later = (
        qkv_weight,
        swapped,
        jnp.asarray(cosine),
        jnp.asarray(sine),
        heads,
        out_weight,
        grads,
    )
    return pl.pallas_call(
        lambda *refs: layer_kernel(*refs, factor_all=factor_all),
        out_shape=(
            jax.ShapeDtypeStruct((FRAMES, D), jnp.bfloat16),
            jax.ShapeDtypeStruct((2 * INNER, D), jnp.bfloat16),
            jax.ShapeDtypeStruct((2 * INNER, D), jnp.bfloat16),
        ),
        in_specs=[whole(pltpu.SMEM)] + [whole()] * 3 + [whole(pl.ANY)] * len(later),
        out_specs=(whole(),) * 3,
        scratch_shapes=[pltpu.VMEM(value.shape, value.dtype) for value in later]
        + [
            pltpu.VMEM((FRAMES, INNER), jnp.bfloat16),
            pltpu.VMEM((FRAMES, 3 * INNER), jnp.bfloat16),
            pltpu.VMEM((2, 2 * INNER, D), jnp.bfloat16),
            pltpu.SemaphoreType.DMA((len(later),)),
        ],
        name="layer",
    )(core, feats, embed, norm_gain.reshape(1, D), *later)


def unpack(core, half, filled=()):
    return pl.pallas_call(
        unpack_kernel,
        out_shape=(
            jax.ShapeDtypeStruct((D, 3 * INNER), jnp.float32),
            jax.ShapeDtypeStruct((INNER, D), jnp.float32),
        ),
        in_specs=[whole(pltpu.SMEM), whole()] + [whole(pl.ANY)] * len(filled),
        out_specs=(whole(pl.ANY),) * 2,
        input_output_aliases={2 + at: at for at in range(len(filled))},
        scratch_shapes=[
            pltpu.VMEM((D // 2, 3 * INNER), jnp.float32),
            pltpu.VMEM((INNER // 2, D), jnp.float32),
            pltpu.SemaphoreType.DMA((2,)),
        ],
        name="unpack",
    )(core, half, *filled)


def exchange(blocks, axis):
    return lax.all_to_all(blocks, axis, split_axis=0, concat_axis=0, tiled=True)


def reduced(blocks):
    return jnp.sum(blocks.astype(jnp.float32), axis=0).astype(jnp.bfloat16)


def scatter_sum(values, axis):
    count = lax.axis_size(axis)
    blocks = values.reshape(count, values.shape[0] // count, values.shape[1])
    return reduced(exchange(blocks, axis))


def gather(values, axis):
    count = lax.axis_size(axis)
    blocks = jnp.broadcast_to(values[None], (count,) + values.shape)
    return exchange(blocks, axis).reshape(count * values.shape[0], values.shape[1])


def staged(
    audio_clips, band_widths, band_gain, band_weight, norm_gain, qkv_weight, out_weight, cotangent
):
    tm = lax.axis_size(TIME)
    band_at = lax.axis_index("x") * lax.axis_size("core") + lax.axis_index("core")
    own_bands = band_gain.shape[0]
    frame_block = audio_clips.shape[2] // HOP
    rim = lax.ppermute(audio_clips, TIME, [(source, source - 1) for source in range(1, tm)])
    sequences = own_bands * CLIPS
    rows = FEAT // tm
    early = jnp.concatenate(
        [
            cotangent.reshape(sequences, frame_block, D),
            jnp.broadcast_to(band_weight[:, None], (own_bands, CLIPS, rows, D)).reshape(
                sequences, rows, D
            ),
        ],
        axis=1,
    )
    early = exchange(early, TIME)
    grads = early[:, :frame_block].reshape(FRAMES, D)
    weight = early[:, frame_block:].reshape(FEAT, D)
    normed = spectrum(band_at, band_widths, audio_clips, rim, band_gain)
    feats = exchange(normed, TIME).reshape(FRAMES, FEAT)
    factor_all = 1.0 / math.sqrt(BANDS * CLIPS * FRAMES)
    core = lax.axis_index("core").reshape(1)
    prepared = prepare(weight, grads, qkv_weight, out_weight)
    attended, keep, send = layer(
        core, feats, prepared, grads, norm_gain, qkv_weight, out_weight, factor_all
    )
    swap = [(0, 1), (1, 0)]
    partial = keep.astype(jnp.float32) + lax.ppermute(send, "core", swap).astype(jnp.float32)
    partial = scatter_sum(partial.astype(jnp.bfloat16), "x")
    both = jnp.concatenate(
        [attended.reshape(tm, frame_block, D), partial.reshape(tm, -1, D)], axis=1
    )
    both = exchange(both, TIME)
    attended_out = both[:, :frame_block].reshape(own_bands, CLIPS, frame_block, D)
    partial = gather(gather(reduced(both[:, frame_block:]), TIME), "x")
    other = lax.ppermute(partial, "core", swap)
    filled = unpack(core, partial)
    grad_qkv, grad_out = unpack(1 - core, other, filled)
    return (attended_out, grad_qkv, grad_out)


def solution(mesh):
    split = Mesh(mesh.devices.reshape(8, -1, 4, 2), TIME + BAND)
    return jax.shard_map(
        staged,
        mesh=split,
        in_specs=(
            P(None, None, TIME),
            P(),
            P(BAND, None),
            P(BAND, TIME, None),
            P(),
            P(),
            P(),
            P(BAND, None, TIME, None),
        ),
        out_specs=(P(BAND, None, TIME, None), P(), P()),
        check_vma=False,
    )
```

```python
import math

import jax
import jax.numpy as jnp
import numpy as np
from jax import lax
from jax.experimental import pallas as pl
from jax.experimental.pallas import tpu as pltpu
from jax.sharding import Mesh, PartitionSpec as P


D = 384
HEADS = 8
HDIM = 64
WIN = 2048
HOP = 441
BANDS = 64
MAXW = 128
CLIPS = 8
INNER = 512
BINS = 1024
FEAT = 512
FRAMES = 256
TIME = ("z", "y")
BAND = ("x", "core")

OUTER = 8
SPAN = WIN // OUTER
HIGH = BINS // OUTER


def window_table():
    sample_at = np.arange(WIN, dtype=np.float64)
    taper = (0.5 - 0.5 * np.cos(sample_at * (2.0 * np.pi / WIN))) / np.sqrt(WIN)
    return taper.reshape(1, WIN).astype(np.float32)


def twiddle_table():
    phase = np.outer(np.arange(OUTER), np.arange(SPAN)) % WIN
    angle = phase * (2.0 * np.pi / WIN)
    return np.concatenate([np.cos(angle), np.sin(angle)], axis=0).astype(np.float32)


def inner_table():
    phase = np.outer(np.arange(SPAN), np.arange(HIGH)) % SPAN
    angle = phase * (2.0 * np.pi / SPAN)
    real, imag = np.cos(angle), np.sin(angle)
    return np.concatenate(
        [np.concatenate([real, -imag], axis=1), np.concatenate([imag, real], axis=1)], axis=0
    ).astype(np.float32)


def rotary_table(frame_order):
    freq = np.exp(np.arange(HDIM // 2, dtype=np.float32) * np.float32(-2.0 * math.log(10000.0) / HDIM))
    angle = (frame_order.astype(np.float32)[:, None] * freq.astype(np.float32)[None, :]).astype(np.float64)
    cosine, sine = np.cos(angle), np.sin(angle)
    return (
        np.concatenate([cosine] * 4, axis=1).astype(np.float32),
        np.concatenate([-sine, sine, -sine, sine], axis=1).astype(np.float32),
    )


def split_bf16(values):
    parts = []
    for _ in range(3):
        kept = values.astype(jnp.bfloat16)
        parts.append(kept)
        values = values - kept.astype(jnp.float32)
    return parts


def one_hot(hit):
    return jnp.where(hit, 1.0, 0.0).astype(jnp.bfloat16)


def spectrum_kernel(
    place_ref,
    widths_ref,
    audio_ref,
    rim_ref,
    gain_ref,
    taper_ref,
    twiddle_ref,
    inner_ref,
    out_ref,
    lead,
    tail,
    framed,
    stage,
    bins,
    pick,
):
    own = audio_ref.shape[2]
    rows = audio_ref.shape[0] * audio_ref.shape[1]
    frames_here = own // HOP
    total = rows * frames_here
    own_bands = gain_ref.shape[0]
    for c in range(CLIPS):
        lead[2 * c : 2 * c + 2, :own] = audio_ref[c]
        tail[2 * c : 2 * c + 2, :own] = rim_ref[c]
    lane = lax.broadcasted_iota(jnp.int32, (rows, WIN), 1)
    for f in range(frames_here):
        here = own - HOP * f
        head = lead[...] if f == 0 else pltpu.roll(lead[...], WIN - HOP * f, 1)
        rest = pltpu.roll(tail[...], here % WIN, 1)
        frame = jnp.where(lane < here, head, rest) * taper_ref[...]
        for block in range(WIN // 128):
            framed[block, pl.ds(f, rows, stride=frames_here), :] = frame[
                :, block * 128 : (block + 1) * 128
            ]
    root = math.sqrt(0.5)
    for half in range(SPAN // 128):
        x = [framed[2 * n + half] for n in range(OUTER)]
        e0, e1, e2, e3 = x[0] + x[4], x[1] + x[5], x[2] + x[6], x[3] + x[7]
        d0, d1, d2, d3 = x[0] - x[4], x[1] - x[5], x[2] - x[6], x[3] - x[7]
        s02, s13 = e0 + e2, e1 + e3
        p = (d1 - d3) * root
        q = (d1 + d3) * root
        real = [s02 + s13, d0 + p, e0 - e2, d0 - p, s02 - s13]
        imag = [None, -(q + d2), e3 - e1, d2 - q, None]
        lanes = slice(half * 128, (half + 1) * 128)
        for low in range(OUTER):
            if low <= 4:
                re, im = real[low], imag[low]
            else:
                re, im = real[8 - low], -imag[8 - low]
            at = slice(low * total, (low + 1) * total)
            if low == 0:
                stage[at, half * 128 : (half + 1) * 128] = re
                stage[at, SPAN + half * 128 : SPAN + (half + 1) * 128] = jnp.zeros_like(re)
                continue
            c = twiddle_ref[low : low + 1, lanes]
            s = twiddle_ref[OUTER + low : OUTER + low + 1, lanes]
            if im is None:
                zr, zi = re * c, -(re * s)
            else:
                zr, zi = re * c + im * s, im * c - re * s
            stage[at, half * 128 : (half + 1) * 128] = zr
            stage[at, SPAN + half * 128 : SPAN + (half + 1) * 128] = zi
    made = jnp.dot(
        stage[...],
        inner_ref[...],
        preferred_element_type=jnp.float32,
        precision=lax.Precision.HIGHEST,
    )
    for low in range(OUTER):
        cols = slice(low * HIGH, (low + 1) * HIGH)
        for part in range(2):
            piece = made[low * total : (low + 1) * total, part * HIGH : (part + 1) * HIGH]
            for split, kept in enumerate(split_bf16(piece)):
                at = (split * 2 + part) * total
                bins[at : at + total, cols] = kept
    first_band = place_ref[0] * own_bands
    start = lax.fori_loop(0, first_band, lambda i, past: past + widths_ref[i], jnp.int32(0))
    within = lax.broadcasted_iota(jnp.int32, (1, MAXW), 1)
    high_at = OUTER * lax.broadcasted_iota(jnp.int32, (HIGH, MAXW), 0)
    counts = []
    for band in range(own_bands):
        width = widths_ref[first_band + band]
        target = jnp.where(within < width, start + within, -1)
        for low in range(OUTER):
            pick[low * HIGH : (low + 1) * HIGH, band * MAXW : (band + 1) * MAXW] = one_hot(
                high_at == target - low
            )
        counts.append((4 * width).astype(jnp.float32))
        start = start + width
    chosen = jnp.dot(bins[...], pick[...], preferred_element_type=jnp.float32)
    exact = chosen[: 2 * total] + chosen[2 * total : 4 * total] + chosen[4 * total :]
    feature = lax.broadcasted_iota(jnp.int32, (FEAT, FEAT), 0)
    column = lax.broadcasted_iota(jnp.int32, (FEAT, FEAT), 1)
    order = one_hot(feature == (column % MAXW) * 4 + column // MAXW)
    gain = sum(
        jnp.dot(part, order, preferred_element_type=jnp.float32)
        for part in split_bf16(gain_ref[...])
    )
    row = lax.broadcasted_iota(jnp.int32, (total, 1), 0)
    for band in range(own_bands):
        cols = slice(band * MAXW, (band + 1) * MAXW)
        re = exact[:total, cols]
        im = exact[total:, cols]
        power = jnp.sum(re * re + im * im, axis=1, keepdims=True)
        ahead = pltpu.roll(power, total - frames_here, 0)
        behind = pltpu.roll(power, frames_here, 0)
        power = power + jnp.where(row % (2 * frames_here) < frames_here, ahead, behind)
        inverse = lax.rsqrt(jnp.maximum(power / counts[band], 0.25))
        for r in range(2):
            value = ((re, im)[r] * inverse).reshape(CLIPS, 2 * frames_here, MAXW)
            for a in range(2):
                which = 2 * a + r
                lanes = slice(which * MAXW, (which + 1) * MAXW)
                own_gain = gain[band : band + 1, lanes]
                out_ref[band * CLIPS : (band + 1) * CLIPS, :, lanes] = (
                    value[:, a * frames_here : (a + 1) * frames_here, :] * own_gain[None]
                ).astype(jnp.bfloat16)


def assemble_kernel(grads_ref, weight_ref, out_ref):
    block = grads_ref.shape[1]
    steps = weight_ref.shape[1] // block
    out_ref[:, 0] = grads_ref[...]
    for band in range(weight_ref.shape[0]):
        for step in range(steps):
            piece = weight_ref[band, step * block : (step + 1) * block, :]
            for c in range(CLIPS):
                out_ref[band * CLIPS + c, 1 + step] = piece


def dot(left, right, dims=((1,), (0,))):
    return lax.dot_general(left, right, (dims, ((), ())), preferred_element_type=jnp.float32)


def split_heads(values):
    low = lax.broadcasted_iota(jnp.int32, values.shape, 1) < HDIM
    return (
        jnp.where(low, values, 0.0).astype(jnp.bfloat16),
        jnp.where(low, 0.0, values).astype(jnp.bfloat16),
    )


def prepare_kernel(weight_ref, grads_ref, qkv_ref, outw_ref, embed_ref, heads_ref, swapped_ref):
    natural = lax.broadcasted_iota(jnp.int32, (FEAT, FEAT), 1)
    wanted = lax.broadcasted_iota(jnp.int32, (FEAT, FEAT), 0)
    order = one_hot(natural == (wanted % MAXW) * 4 + wanted // MAXW)
    embed_ref[...] = dot(order, weight_ref[...]).astype(jnp.bfloat16)
    grad_mixed = dot(grads_ref[...], outw_ref[...], ((1,), (1,)))
    for pair in range(HEADS // 2):
        low, high = split_heads(grad_mixed[:, pair * 128 : (pair + 1) * 128])
        heads_ref[pair, :FRAMES, :] = low
        heads_ref[pair, FRAMES:, :] = high
    row = lax.broadcasted_iota(jnp.int32, (128, 128), 0)
    lane = lax.broadcasted_iota(jnp.int32, (128, 128), 1)
    swap = one_hot(row == lane + jnp.where(lane % HDIM < HDIM // 2, HDIM // 2, -(HDIM // 2)))
    for block in range(2 * INNER // 128):
        cols = slice(block * 128, (block + 1) * 128)
        swapped_ref[:, cols] = dot(qkv_ref[:, cols], swap).astype(jnp.bfloat16)


def layer_kernel(
    core_ref,
    feats_ref,
    embed_ref,
    gain_ref,
    qkv_hbm,
    swapped_hbm,
    cos_hbm,
    sin_hbm,
    heads_hbm,
    outw_hbm,
    grads_hbm,
    attended_ref,
    keep_ref,
    send_ref,
    qkv_ref,
    swapped_ref,
    cos_ref,
    sin_ref,
    heads_ref,
    outw_ref,
    grads_ref,
    mixed_s,
    gproj_s,
    halves,
    sems,
    *,
    factor_all,
):
    pairs = (
        (qkv_hbm, qkv_ref),
        (swapped_hbm, swapped_ref),
        (cos_hbm, cos_ref),
        (sin_hbm, sin_ref),
        (heads_hbm, heads_ref),
        (outw_hbm, outw_ref),
        (grads_hbm, grads_ref),
    )
    copies = [
        pltpu.make_async_copy(source, target, sems.at[at])
        for at, (source, target) in enumerate(pairs)
    ]
    for copy in copies:
        copy.start()
    x = dot(feats_ref[...].reshape(FRAMES, FEAT), embed_ref[...]).astype(jnp.bfloat16).astype(jnp.float32)
    scale = lax.rsqrt(jnp.mean(x * x, axis=1, keepdims=True) + 1e-06)
    normed_x = (x * scale * gain_ref[...]).astype(jnp.bfloat16)
    for copy in copies[:4]:
        copy.wait()
    factor = 1.0 / math.sqrt(HDIM)
    cosine = cos_ref[...]
    sine = sin_ref[...]
    for copy in copies[4:]:
        copy.wait()

    def opened(pair):
        cols = slice(pair * 128, (pair + 1) * 128)
        after = slice(INNER + pair * 128, INNER + (pair + 1) * 128)
        q, k, v = (
            dot(normed_x, qkv_ref[:, part * INNER + pair * 128 : part * INNER + (pair + 1) * 128])
            for part in range(3)
        )
        q_swap = dot(normed_x, swapped_ref[:, cols])
        k_swap = dot(normed_x, swapped_ref[:, after])
        query = split_heads((q * cosine + q_swap * sine) * factor)
        query_swap = split_heads((q_swap * cosine - q * sine) * factor)
        turned = k * cosine + k_swap * sine
        key = split_heads(turned)
        key_swap = split_heads(k_swap * cosine - k * sine)
        value = split_heads(v)
        stacked = jnp.concatenate(query, axis=0)
        scores = dot(stacked, turned.astype(jnp.bfloat16), ((1,), (1,)))
        grad_p = dot(heads_ref[pair], v.astype(jnp.bfloat16), ((1,), (1,)))
        both_q = jnp.concatenate([stacked, jnp.concatenate(query_swap, axis=0)], axis=1)
        both_k = [jnp.concatenate([a, b], axis=1) for a, b in zip(key, key_swap)]
        return scores, grad_p, both_q, both_k, value

    def closed(pair, scores, grad_p, both_q, both_k, value):
        cols = slice(pair * 128, (pair + 1) * 128)
        peak = jnp.max(scores, axis=1, keepdims=True)
        expo = jnp.exp(scores - peak)
        probs = expo / jnp.sum(expo, axis=1, keepdims=True)
        probs_b = probs.astype(jnp.bfloat16)
        row_dot = jnp.sum(probs * grad_p, axis=1, keepdims=True)
        grad_s = (probs * (grad_p - row_dot)).astype(jnp.bfloat16)
        mixed = dot(probs_b[:FRAMES], value[0]) + dot(probs_b[FRAMES:], value[1])
        grad_v = dot(probs_b, heads_ref[pair], ((0,), (0,)))
        grad_q = (dot(grad_s[:FRAMES], both_k[0]) + dot(grad_s[FRAMES:], both_k[1])) * factor
        grad_k = dot(grad_s, both_q, ((0,), (0,)))
        mixed_s[:, cols] = mixed.astype(jnp.bfloat16)
        for part, grad in enumerate((grad_q, grad_k)):
            turned = grad[:, :128] * cosine - grad[:, 128:] * sine
            gproj_s[:, part * INNER + pair * 128 : part * INNER + (pair + 1) * 128] = turned.astype(
                jnp.bfloat16
            )
        gproj_s[:, 2 * INNER + pair * 128 : 2 * INNER + (pair + 1) * 128] = grad_v.astype(
            jnp.bfloat16
        )

    ready = opened(0)
    for pair in range(HEADS // 2):
        following = opened(pair + 1) if pair + 1 < HEADS // 2 else None
        closed(pair, *ready)
        ready = following
    mixed_b = mixed_s[...]
    attended = x + dot(mixed_b, outw_ref[...])
    attended_ref[...] = attended.reshape(attended_ref.shape).astype(jnp.bfloat16)
    core = core_ref[0]

    def place(first, values):
        values = (values * factor_all).astype(jnp.bfloat16)
        rows = values.shape[0] // 2
        halves[core, first : first + rows, :] = values[:rows]
        halves[1 - core, first : first + rows, :] = values[rows:]

    for block in range(3 * INNER // D):
        place(
            block * D // 2, dot(normed_x, gproj_s[:, block * D : (block + 1) * D], ((0,), (0,)))
        )
    place(3 * INNER // 2, dot(mixed_b, grads_ref[...], ((0,), (0,))))
    keep_ref[...] = halves[0]
    send_ref[...] = halves[1]


def unpack_kernel(core_ref, half_ref, *refs):
    grad_qkv_hbm, grad_out_hbm, wide, tall, sems = refs[-5:]
    rows = wide.shape[0]
    for block in range(3 * INNER // D):
        wide[:, block * D : (block + 1) * D] = half_ref[
            block * rows : (block + 1) * rows, :
        ].astype(jnp.float32)
    tall[...] = half_ref[3 * INNER // D * rows :, :].astype(jnp.float32)
    core = core_ref[0]
    copies = []
    for at, (source, target) in enumerate(((wide, grad_qkv_hbm), (tall, grad_out_hbm))):
        count = source.shape[0]
        place = target.at[pl.ds(pl.multiple_of(core * count, count), count), :]
        copies.append(pltpu.make_async_copy(source, place, sems.at[at]))
    for copy in copies:
        copy.start()
    for copy in copies:
        copy.wait()


def whole(memory_space=pltpu.VMEM):
    return pl.BlockSpec(memory_space=memory_space)


def spectrum(band_at, band_widths, audio, rim, gain):
    rows, own = audio.shape[0] * audio.shape[1], audio.shape[2]
    frames_here = own // HOP
    total = rows * frames_here
    own_bands = gain.shape[0]
    return pl.pallas_call(
        spectrum_kernel,
        out_shape=jax.ShapeDtypeStruct((own_bands * CLIPS, frames_here, FEAT), jnp.bfloat16),
        in_specs=[whole(pltpu.SMEM)] * 2 + [whole()] * 6,
        out_specs=whole(),
        scratch_shapes=[
            pltpu.VMEM((rows, WIN), jnp.float32),
            pltpu.VMEM((rows, WIN), jnp.float32),
            pltpu.VMEM((WIN // 128, total, 128), jnp.float32),
            pltpu.VMEM((OUTER * total, 2 * SPAN), jnp.float32),
            pltpu.VMEM((6 * total, BINS), jnp.bfloat16),
            pltpu.VMEM((BINS, own_bands * MAXW), jnp.bfloat16),
        ],
        name="spectrum",
    )(
        band_at.reshape(1),
        band_widths,
        audio,
        rim,
        gain,
        jnp.asarray(window_table()),
        jnp.asarray(twiddle_table()),
        jnp.asarray(inner_table()),
    )


def assemble(grads, weight):
    sequences, block, width = grads.shape
    return pl.pallas_call(
        assemble_kernel,
        out_shape=jax.ShapeDtypeStruct(
            (sequences, 1 + weight.shape[1] // block, block, width), grads.dtype
        ),
        in_specs=[whole()] * 2,
        out_specs=whole(),
        name="assemble",
    )(grads, weight)


def prepare(weight, grads, qkv_weight, out_weight):
    return pl.pallas_call(
        prepare_kernel,
        out_shape=(
            jax.ShapeDtypeStruct((FEAT, D), jnp.bfloat16),
            jax.ShapeDtypeStruct((HEADS // 2, 2 * FRAMES, 128), jnp.bfloat16),
            jax.ShapeDtypeStruct((D, 2 * INNER), jnp.bfloat16),
        ),
        in_specs=[whole()] * 4,
        out_specs=(whole(),) * 3,
        name="prepare",
    )(weight, grads, qkv_weight, out_weight)


def layer(core, feats, prepared, grads, norm_gain, qkv_weight, out_weight, factor_all):
    embed, heads, swapped = prepared
    cosine, sine = rotary_table(np.arange(FRAMES))
    later = (
        qkv_weight,
        swapped,
        jnp.asarray(cosine),
        jnp.asarray(sine),
        heads,
        out_weight,
        grads,
    )
    return pl.pallas_call(
        lambda *refs: layer_kernel(*refs, factor_all=factor_all),
        out_shape=(
            jax.ShapeDtypeStruct(feats.shape[:2] + (D,), jnp.bfloat16),
            jax.ShapeDtypeStruct((2 * INNER, D), jnp.bfloat16),
            jax.ShapeDtypeStruct((2 * INNER, D), jnp.bfloat16),
        ),
        in_specs=[whole(pltpu.SMEM)] + [whole()] * 3 + [whole(pl.ANY)] * len(later),
        out_specs=(whole(),) * 3,
        scratch_shapes=[pltpu.VMEM(value.shape, value.dtype) for value in later]
        + [
            pltpu.VMEM((FRAMES, INNER), jnp.bfloat16),
            pltpu.VMEM((FRAMES, 3 * INNER), jnp.bfloat16),
            pltpu.VMEM((2, 2 * INNER, D), jnp.bfloat16),
            pltpu.SemaphoreType.DMA((len(later),)),
        ],
        name="layer",
    )(core, feats, embed, norm_gain.reshape(1, D), *later)


def unpack(core, half, filled=()):
    return pl.pallas_call(
        unpack_kernel,
        out_shape=(
            jax.ShapeDtypeStruct((D, 3 * INNER), jnp.float32),
            jax.ShapeDtypeStruct((INNER, D), jnp.float32),
        ),
        in_specs=[whole(pltpu.SMEM), whole()] + [whole(pl.ANY)] * len(filled),
        out_specs=(whole(pl.ANY),) * 2,
        input_output_aliases={2 + at: at for at in range(len(filled))},
        scratch_shapes=[
            pltpu.VMEM((D // 2, 3 * INNER), jnp.float32),
            pltpu.VMEM((INNER // 2, D), jnp.float32),
            pltpu.SemaphoreType.DMA((2,)),
        ],
        name="unpack",
    )(core, half, *filled)


def exchange(blocks, axis):
    return lax.all_to_all(blocks, axis, split_axis=0, concat_axis=0, tiled=True)


def reduced(blocks):
    return jnp.sum(blocks.astype(jnp.float32), axis=0).astype(jnp.bfloat16)


def scatter_sum(values, axis):
    count = lax.axis_size(axis)
    blocks = values.reshape(count, values.shape[0] // count, values.shape[1])
    return reduced(exchange(blocks, axis))


def gather(values, axis):
    count = lax.axis_size(axis)
    blocks = jnp.broadcast_to(values[None], (count,) + values.shape)
    return exchange(blocks, axis).reshape(count * values.shape[0], values.shape[1])


def staged(
    audio_clips, band_widths, band_gain, band_weight, norm_gain, qkv_weight, out_weight, cotangent
):
    tm = lax.axis_size(TIME)
    band_at = lax.axis_index("x") * lax.axis_size("core") + lax.axis_index("core")
    own_bands = band_gain.shape[0]
    frame_block = audio_clips.shape[2] // HOP
    rim = lax.ppermute(audio_clips, TIME, [(source, source - 1) for source in range(1, tm)])
    sequences = own_bands * CLIPS
    early = assemble(cotangent.reshape(sequences, frame_block, D), band_weight)
    parts = early.shape[1]
    early = exchange(early.reshape(sequences * parts, frame_block, D), TIME)
    early = early.reshape(tm, parts, frame_block, D)
    grads = early[:, 0].reshape(FRAMES, D)
    weight = early[:, 1:].reshape(FEAT, D)
    normed = spectrum(band_at, band_widths, audio_clips, rim, band_gain)
    feats = exchange(normed, TIME)
    factor_all = 1.0 / math.sqrt(BANDS * CLIPS * FRAMES)
    core = lax.axis_index("core").reshape(1)
    prepared = prepare(weight, grads, qkv_weight, out_weight)
    attended, keep, send = layer(
        core, feats, prepared, grads, norm_gain, qkv_weight, out_weight, factor_all
    )
    swap = [(0, 1), (1, 0)]
    partial = keep.astype(jnp.float32) + lax.ppermute(send, "core", swap).astype(jnp.float32)
    partial = scatter_sum(partial.astype(jnp.bfloat16), "x")
    both = jnp.concatenate(
        [attended, partial.reshape(tm, -1, D)], axis=1
    )
    both = exchange(both, TIME)
    attended_out = both[:, :frame_block].reshape(own_bands, CLIPS, frame_block, D)
    partial = gather(gather(reduced(both[:, frame_block:]), TIME), "x")
    other = lax.ppermute(partial, "core", swap)
    filled = unpack(core, partial)
    grad_qkv, grad_out = unpack(1 - core, other, filled)
    return (attended_out, grad_qkv, grad_out)


def solution(mesh):
    split = Mesh(mesh.devices.reshape(8, -1, 4, 2), TIME + BAND)
    return jax.shard_map(
        staged,
        mesh=split,
        in_specs=(
            P(None, None, TIME),
            P(),
            P(BAND, None),
            P(BAND, TIME, None),
            P(),
            P(),
            P(),
            P(BAND, None, TIME, None),
        ),
        out_specs=(P(BAND, None, TIME, None), P(), P()),
        check_vma=False,
    )
```

```python
import math

import jax
import jax.numpy as jnp
import numpy as np
from jax import lax
from jax.experimental import pallas as pl
from jax.experimental.pallas import tpu as pltpu
from jax.sharding import Mesh, PartitionSpec as P


D = 384
HEADS = 8
HDIM = 64
WIN = 2048
HOP = 441
BANDS = 64
MAXW = 128
CLIPS = 8
INNER = 512
BINS = 1024
FEAT = 512
FRAMES = 256
TIME = ("z", "y")
BAND = ("x", "core")

OUTER = 8
SPAN = WIN // OUTER
HIGH = BINS // OUTER


def window_table():
    sample_at = np.arange(WIN, dtype=np.float64)
    taper = (0.5 - 0.5 * np.cos(sample_at * (2.0 * np.pi / WIN))) / np.sqrt(WIN)
    return taper.reshape(1, WIN).astype(np.float32)


def twiddle_table():
    phase = np.outer(np.arange(OUTER), np.arange(SPAN)) % WIN
    angle = phase * (2.0 * np.pi / WIN)
    return np.concatenate([np.cos(angle), np.sin(angle)], axis=0).astype(np.float32)


def inner_table():
    phase = np.outer(np.arange(SPAN), np.arange(HIGH)) % SPAN
    angle = phase * (2.0 * np.pi / SPAN)
    real, imag = np.cos(angle), np.sin(angle)
    return np.concatenate(
        [np.concatenate([real, -imag], axis=1), np.concatenate([imag, real], axis=1)], axis=0
    ).astype(np.float32)


def rotary_table(frame_order):
    freq = np.exp(np.arange(HDIM // 2, dtype=np.float32) * np.float32(-2.0 * math.log(10000.0) / HDIM))
    angle = (frame_order.astype(np.float32)[:, None] * freq.astype(np.float32)[None, :]).astype(np.float64)
    cosine, sine = np.cos(angle), np.sin(angle)
    return (
        np.concatenate([cosine] * 4, axis=1).astype(np.float32),
        np.concatenate([-sine, sine, -sine, sine], axis=1).astype(np.float32),
    )


def split_bf16(values):
    parts = []
    for _ in range(3):
        kept = values.astype(jnp.bfloat16)
        parts.append(kept)
        values = values - kept.astype(jnp.float32)
    return parts


def one_hot(hit):
    return jnp.where(hit, 1.0, 0.0).astype(jnp.bfloat16)


def spectrum_kernel(
    place_ref,
    widths_ref,
    audio_ref,
    rim_ref,
    gain_ref,
    taper_ref,
    twiddle_ref,
    inner_ref,
    out_ref,
    lead,
    tail,
    framed,
    stage,
    bins,
    pick,
):
    own = audio_ref.shape[2]
    rows = audio_ref.shape[0] * audio_ref.shape[1]
    frames_here = own // HOP
    total = rows * frames_here
    own_bands = gain_ref.shape[0]
    for c in range(CLIPS):
        lead[2 * c : 2 * c + 2, :own] = audio_ref[c]
        tail[2 * c : 2 * c + 2, :own] = rim_ref[c]
    lane = lax.broadcasted_iota(jnp.int32, (rows, WIN), 1)
    for f in range(frames_here):
        here = own - HOP * f
        head = lead[...] if f == 0 else pltpu.roll(lead[...], WIN - HOP * f, 1)
        rest = pltpu.roll(tail[...], here % WIN, 1)
        frame = jnp.where(lane < here, head, rest) * taper_ref[...]
        for block in range(WIN // 128):
            framed[block, pl.ds(f, rows, stride=frames_here), :] = frame[
                :, block * 128 : (block + 1) * 128
            ]
    root = math.sqrt(0.5)
    for half in range(SPAN // 128):
        x = [framed[2 * n + half] for n in range(OUTER)]
        e0, e1, e2, e3 = x[0] + x[4], x[1] + x[5], x[2] + x[6], x[3] + x[7]
        d0, d1, d2, d3 = x[0] - x[4], x[1] - x[5], x[2] - x[6], x[3] - x[7]
        s02, s13 = e0 + e2, e1 + e3
        p = (d1 - d3) * root
        q = (d1 + d3) * root
        real = [s02 + s13, d0 + p, e0 - e2, d0 - p, s02 - s13]
        imag = [None, -(q + d2), e3 - e1, d2 - q, None]
        lanes = slice(half * 128, (half + 1) * 128)
        for low in range(OUTER):
            if low <= 4:
                re, im = real[low], imag[low]
            else:
                re, im = real[8 - low], -imag[8 - low]
            at = slice(low * total, (low + 1) * total)
            if low == 0:
                stage[at, half * 128 : (half + 1) * 128] = re
                stage[at, SPAN + half * 128 : SPAN + (half + 1) * 128] = jnp.zeros_like(re)
                continue
            c = twiddle_ref[low : low + 1, lanes]
            s = twiddle_ref[OUTER + low : OUTER + low + 1, lanes]
            if im is None:
                zr, zi = re * c, -(re * s)
            else:
                zr, zi = re * c + im * s, im * c - re * s
            stage[at, half * 128 : (half + 1) * 128] = zr
            stage[at, SPAN + half * 128 : SPAN + (half + 1) * 128] = zi
    made = jnp.dot(
        stage[...],
        inner_ref[...],
        preferred_element_type=jnp.float32,
        precision=lax.Precision.HIGHEST,
    )
    for low in range(OUTER):
        cols = slice(low * HIGH, (low + 1) * HIGH)
        for part in range(2):
            piece = made[low * total : (low + 1) * total, part * HIGH : (part + 1) * HIGH]
            for split, kept in enumerate(split_bf16(piece)):
                at = (split * 2 + part) * total
                bins[at : at + total, cols] = kept
    first_band = place_ref[0] * own_bands
    start = lax.fori_loop(0, first_band, lambda i, past: past + widths_ref[i], jnp.int32(0))
    within = lax.broadcasted_iota(jnp.int32, (1, MAXW), 1)
    high_at = OUTER * lax.broadcasted_iota(jnp.int32, (HIGH, MAXW), 0)
    counts = []
    for band in range(own_bands):
        width = widths_ref[first_band + band]
        target = jnp.where(within < width, start + within, -1)
        for low in range(OUTER):
            pick[low * HIGH : (low + 1) * HIGH, band * MAXW : (band + 1) * MAXW] = one_hot(
                high_at == target - low
            )
        counts.append((4 * width).astype(jnp.float32))
        start = start + width
    chosen = jnp.dot(bins[...], pick[...], preferred_element_type=jnp.float32)
    exact = chosen[: 2 * total] + chosen[2 * total : 4 * total] + chosen[4 * total :]
    feature = lax.broadcasted_iota(jnp.int32, (FEAT, FEAT), 0)
    column = lax.broadcasted_iota(jnp.int32, (FEAT, FEAT), 1)
    order = one_hot(feature == (column % MAXW) * 4 + column // MAXW)
    gain = sum(
        jnp.dot(part, order, preferred_element_type=jnp.float32)
        for part in split_bf16(gain_ref[...])
    )
    row = lax.broadcasted_iota(jnp.int32, (total, 1), 0)
    for band in range(own_bands):
        cols = slice(band * MAXW, (band + 1) * MAXW)
        re = exact[:total, cols]
        im = exact[total:, cols]
        power = jnp.sum(re * re + im * im, axis=1, keepdims=True)
        ahead = pltpu.roll(power, total - frames_here, 0)
        behind = pltpu.roll(power, frames_here, 0)
        power = power + jnp.where(row % (2 * frames_here) < frames_here, ahead, behind)
        inverse = lax.rsqrt(jnp.maximum(power / counts[band], 0.25))
        for r in range(2):
            value = ((re, im)[r] * inverse).reshape(CLIPS, 2 * frames_here, MAXW)
            for a in range(2):
                which = 2 * a + r
                lanes = slice(which * MAXW, (which + 1) * MAXW)
                own_gain = gain[band : band + 1, lanes]
                out_ref[band * CLIPS : (band + 1) * CLIPS, :, lanes] = (
                    value[:, a * frames_here : (a + 1) * frames_here, :] * own_gain[None]
                ).astype(jnp.bfloat16)


def assemble_kernel(grads_ref, weight_ref, out_ref):
    block = grads_ref.shape[1]
    steps = weight_ref.shape[1] // block
    out_ref[:, 0] = grads_ref[...]
    for band in range(weight_ref.shape[0]):
        for step in range(steps):
            piece = weight_ref[band, step * block : (step + 1) * block, :]
            for c in range(CLIPS):
                out_ref[band * CLIPS + c, 1 + step] = piece


def dot(left, right, dims=((1,), (0,))):
    return lax.dot_general(left, right, (dims, ((), ())), preferred_element_type=jnp.float32)


def split_heads(values):
    low = lax.broadcasted_iota(jnp.int32, values.shape, 1) < HDIM
    return (
        jnp.where(low, values, 0.0).astype(jnp.bfloat16),
        jnp.where(low, 0.0, values).astype(jnp.bfloat16),
    )


def prepare_kernel(weight_ref, grads_ref, qkv_ref, outw_ref, embed_ref, heads_ref, turned_ref):
    natural = lax.broadcasted_iota(jnp.int32, (FEAT, FEAT), 1)
    wanted = lax.broadcasted_iota(jnp.int32, (FEAT, FEAT), 0)
    order = one_hot(natural == (wanted % MAXW) * 4 + wanted // MAXW)
    embed_ref[...] = dot(order, weight_ref[...]).astype(jnp.bfloat16)
    grad_mixed = dot(grads_ref[...], outw_ref[...], ((1,), (1,)))
    for pair in range(HEADS // 2):
        low, high = split_heads(grad_mixed[:, pair * 128 : (pair + 1) * 128])
        heads_ref[pair, :FRAMES, :] = low
        heads_ref[pair, FRAMES:, :] = high
    row = lax.broadcasted_iota(jnp.int32, (128, 128), 0)
    lane = lax.broadcasted_iota(jnp.int32, (128, 128), 1)
    swap = one_hot(row == lane + jnp.where(lane % HDIM < HDIM // 2, HDIM // 2, -(HDIM // 2)))
    for part in range(2):
        for pair in range(HEADS // 2):
            piece = qkv_ref[:, part * INNER + pair * 128 : part * INNER + (pair + 1) * 128]
            at = pair * 512 + part * 256
            turned_ref[:, at : at + 128] = piece
            turned_ref[:, at + 128 : at + 256] = dot(piece, swap).astype(jnp.bfloat16)


def layer_kernel(
    core_ref,
    embed_ref,
    gain_ref,
    feats_hbm,
    turned_hbm,
    qkv_hbm,
    cos_hbm,
    sin_hbm,
    heads_hbm,
    outw_hbm,
    grads_hbm,
    attended_ref,
    keep_ref,
    send_ref,
    feats_ref,
    turned_ref,
    plain_ref,
    cos_ref,
    sin_ref,
    heads_ref,
    outw_ref,
    grads_ref,
    mixed_s,
    gproj_s,
    halves,
    sems,
    *,
    factor_all,
):
    pairs = (
        (feats_hbm, feats_ref),
        (turned_hbm, turned_ref),
        (qkv_hbm.at[:, 2 * INNER :], plain_ref),
        (cos_hbm, cos_ref),
        (sin_hbm, sin_ref),
        (heads_hbm, heads_ref),
        (outw_hbm, outw_ref),
        (grads_hbm, grads_ref),
    )
    copies = [
        pltpu.make_async_copy(source, target, sems.at[at])
        for at, (source, target) in enumerate(pairs)
    ]
    for copy in copies:
        copy.start()
    copies[0].wait()
    x = dot(feats_ref[...].reshape(FRAMES, FEAT), embed_ref[...]).astype(jnp.bfloat16).astype(jnp.float32)
    scale = lax.rsqrt(jnp.mean(x * x, axis=1, keepdims=True) + 1e-06)
    normed_x = (x * scale * gain_ref[...]).astype(jnp.bfloat16)
    for copy in copies[1:]:
        copy.wait()
    factor = 1.0 / math.sqrt(HDIM)
    cosine = cos_ref[...]
    sine = sin_ref[...]
    values = dot(normed_x, plain_ref[...])

    def opened(pair):
        made = dot(normed_x, turned_ref[:, pair * 512 : (pair + 1) * 512])
        q, q_swap, k, k_swap = (made[:, at * 128 : (at + 1) * 128] for at in range(4))
        v = values[:, pair * 128 : (pair + 1) * 128]
        query = split_heads((q * cosine + q_swap * sine) * factor)
        query_swap = split_heads((q_swap * cosine - q * sine) * factor)
        turned = k * cosine + k_swap * sine
        key = split_heads(turned)
        key_swap = split_heads(k_swap * cosine - k * sine)
        value = split_heads(v)
        stacked = jnp.concatenate(query, axis=0)
        scores = dot(stacked, turned.astype(jnp.bfloat16), ((1,), (1,)))
        grad_p = dot(heads_ref[pair], v.astype(jnp.bfloat16), ((1,), (1,)))
        both_q = jnp.concatenate([stacked, jnp.concatenate(query_swap, axis=0)], axis=1)
        both_k = [jnp.concatenate([a, b], axis=1) for a, b in zip(key, key_swap)]
        return scores, grad_p, both_q, both_k, value

    def closed(pair, scores, grad_p, both_q, both_k, value):
        cols = slice(pair * 128, (pair + 1) * 128)
        peak = jnp.max(scores, axis=1, keepdims=True)
        expo = jnp.exp(scores - peak)
        probs = expo / jnp.sum(expo, axis=1, keepdims=True)
        probs_b = probs.astype(jnp.bfloat16)
        row_dot = jnp.sum(probs * grad_p, axis=1, keepdims=True)
        grad_s = (probs * (grad_p - row_dot)).astype(jnp.bfloat16)
        mixed = dot(probs_b[:FRAMES], value[0]) + dot(probs_b[FRAMES:], value[1])
        grad_v = dot(probs_b, heads_ref[pair], ((0,), (0,)))
        grad_q = (dot(grad_s[:FRAMES], both_k[0]) + dot(grad_s[FRAMES:], both_k[1])) * factor
        grad_k = dot(grad_s, both_q, ((0,), (0,)))
        mixed_s[:, cols] = mixed.astype(jnp.bfloat16)
        for part, grad in enumerate((grad_q, grad_k)):
            turned = grad[:, :128] * cosine - grad[:, 128:] * sine
            gproj_s[:, part * INNER + pair * 128 : part * INNER + (pair + 1) * 128] = turned.astype(
                jnp.bfloat16
            )
        gproj_s[:, 2 * INNER + pair * 128 : 2 * INNER + (pair + 1) * 128] = grad_v.astype(
            jnp.bfloat16
        )

    ready = opened(0)
    for pair in range(HEADS // 2):
        following = opened(pair + 1) if pair + 1 < HEADS // 2 else None
        closed(pair, *ready)
        ready = following
    mixed_b = mixed_s[...]
    attended = x + dot(mixed_b, outw_ref[...])
    attended_ref[...] = attended.reshape(attended_ref.shape).astype(jnp.bfloat16)
    core = core_ref[0]

    def place(first, values):
        values = (values * factor_all).astype(jnp.bfloat16)
        rows = values.shape[0] // 2
        halves[core, first : first + rows, :] = values[:rows]
        halves[1 - core, first : first + rows, :] = values[rows:]

    for block in range(3 * INNER // D):
        place(
            block * D // 2, dot(normed_x, gproj_s[:, block * D : (block + 1) * D], ((0,), (0,)))
        )
    place(3 * INNER // 2, dot(mixed_b, grads_ref[...], ((0,), (0,))))
    keep_ref[...] = halves[0]
    send_ref[...] = halves[1]


def unpack_kernel(core_ref, half_hbm, *refs):
    grad_qkv_hbm, grad_out_hbm, half_ref, wide_ref, in_sems, out_sems = refs[-6:]
    core = core_ref[0]
    rows = D // 2
    spans = [(at * rows, rows) for at in range(3 * INNER // D)] + [(3 * INNER // 2, INNER // 2)]
    arrivals = []
    for at, (first, count) in enumerate(spans):
        span = pl.ds(first, count)
        arrivals.append(
            pltpu.make_async_copy(half_hbm.at[span, :], half_ref.at[span, :], in_sems.at[at])
        )
    for copy in arrivals:
        copy.start()
    leaving = []
    for at, (first, count) in enumerate(spans):
        arrivals[at].wait()
        span = slice(first, first + count)
        wide_ref[span, :] = half_ref[span, :].astype(jnp.float32)
        place = pl.ds(pl.multiple_of(core * count, count), count)
        if at < len(spans) - 1:
            target = grad_qkv_hbm.at[place, pl.ds(at * D, D)]
        else:
            target = grad_out_hbm.at[place, :]
        leaving.append(
            pltpu.make_async_copy(wide_ref.at[pl.ds(first, count), :], target, out_sems.at[at])
        )
        leaving[-1].start()
    for copy in leaving:
        copy.wait()


def whole(memory_space=pltpu.VMEM):
    return pl.BlockSpec(memory_space=memory_space)


def spectrum(band_at, band_widths, audio, rim, gain):
    rows, own = audio.shape[0] * audio.shape[1], audio.shape[2]
    frames_here = own // HOP
    total = rows * frames_here
    own_bands = gain.shape[0]
    return pl.pallas_call(
        spectrum_kernel,
        out_shape=jax.ShapeDtypeStruct((own_bands * CLIPS, frames_here, FEAT), jnp.bfloat16),
        in_specs=[whole(pltpu.SMEM)] * 2 + [whole()] * 6,
        out_specs=whole(),
        scratch_shapes=[
            pltpu.VMEM((rows, WIN), jnp.float32),
            pltpu.VMEM((rows, WIN), jnp.float32),
            pltpu.VMEM((WIN // 128, total, 128), jnp.float32),
            pltpu.VMEM((OUTER * total, 2 * SPAN), jnp.float32),
            pltpu.VMEM((6 * total, BINS), jnp.bfloat16),
            pltpu.VMEM((BINS, own_bands * MAXW), jnp.bfloat16),
        ],
        name="spectrum",
    )(
        band_at.reshape(1),
        band_widths,
        audio,
        rim,
        gain,
        jnp.asarray(window_table()),
        jnp.asarray(twiddle_table()),
        jnp.asarray(inner_table()),
    )


def assemble(grads, weight):
    sequences, block, width = grads.shape
    return pl.pallas_call(
        assemble_kernel,
        out_shape=jax.ShapeDtypeStruct(
            (sequences, 1 + weight.shape[1] // block, block, width), grads.dtype
        ),
        in_specs=[whole()] * 2,
        out_specs=whole(),
        name="assemble",
    )(grads, weight)


def prepare(weight, grads, qkv_weight, out_weight):
    return pl.pallas_call(
        prepare_kernel,
        out_shape=(
            jax.ShapeDtypeStruct((FEAT, D), jnp.bfloat16),
            jax.ShapeDtypeStruct((HEADS // 2, 2 * FRAMES, 128), jnp.bfloat16),
            jax.ShapeDtypeStruct((D, 4 * INNER), jnp.bfloat16),
        ),
        in_specs=[whole()] * 4,
        out_specs=(whole(),) * 3,
        name="prepare",
    )(weight, grads, qkv_weight, out_weight)


def layer(core, feats, prepared, grads, norm_gain, qkv_weight, out_weight, factor_all):
    embed, heads, turned = prepared
    cosine, sine = rotary_table(np.arange(FRAMES))
    later = (
        feats,
        turned,
        qkv_weight,
        jnp.asarray(cosine),
        jnp.asarray(sine),
        heads,
        out_weight,
        grads,
    )
    return pl.pallas_call(
        lambda *refs: layer_kernel(*refs, factor_all=factor_all),
        out_shape=(
            pltpu.VMEM(feats.shape[:2] + (D,), jnp.bfloat16),
            pltpu.VMEM((2 * INNER, D), jnp.bfloat16),
            pltpu.VMEM((2 * INNER, D), jnp.bfloat16),
        ),
        in_specs=[whole(pltpu.SMEM)] + [whole()] * 2 + [whole(pl.ANY)] * len(later),
        out_specs=(whole(),) * 3,
        scratch_shapes=[
            pltpu.VMEM((D, INNER) if value is qkv_weight else value.shape, value.dtype)
            for value in later
        ]
        + [
            pltpu.VMEM((FRAMES, INNER), jnp.bfloat16),
            pltpu.VMEM((FRAMES, 3 * INNER), jnp.bfloat16),
            pltpu.VMEM((2, 2 * INNER, D), jnp.bfloat16),
            pltpu.SemaphoreType.DMA((len(later),)),
        ],
        name="layer",
    )(core, embed, norm_gain.reshape(1, D), *later)


def unpack(core, half, filled=()):
    return pl.pallas_call(
        unpack_kernel,
        out_shape=(
            jax.ShapeDtypeStruct((D, 3 * INNER), jnp.float32),
            jax.ShapeDtypeStruct((INNER, D), jnp.float32),
        ),
        in_specs=[whole(pltpu.SMEM)] + [whole(pl.ANY)] * (1 + len(filled)),
        out_specs=(whole(pl.ANY),) * 2,
        input_output_aliases={2 + at: at for at in range(len(filled))},
        scratch_shapes=[
            pltpu.VMEM(half.shape, half.dtype),
            pltpu.VMEM(half.shape, jnp.float32),
            pltpu.SemaphoreType.DMA((3 * INNER // D + 1,)),
            pltpu.SemaphoreType.DMA((3 * INNER // D + 1,)),
        ],
        name="unpack",
    )(core, half, *filled)


def exchange(blocks, axis):
    return lax.all_to_all(blocks, axis, split_axis=0, concat_axis=0, tiled=True)


def reduced(blocks):
    return jnp.sum(blocks.astype(jnp.float32), axis=0).astype(jnp.bfloat16)


def scatter_sum(values, axis):
    count = lax.axis_size(axis)
    blocks = values.reshape(count, values.shape[0] // count, values.shape[1])
    return reduced(exchange(blocks, axis))


def gather(values, axis):
    count = lax.axis_size(axis)
    blocks = jnp.broadcast_to(values[None], (count,) + values.shape)
    return exchange(blocks, axis).reshape(count * values.shape[0], values.shape[1])


def staged(
    audio_clips, band_widths, band_gain, band_weight, norm_gain, qkv_weight, out_weight, cotangent
):
    tm = lax.axis_size(TIME)
    band_at = lax.axis_index("x") * lax.axis_size("core") + lax.axis_index("core")
    own_bands = band_gain.shape[0]
    frame_block = audio_clips.shape[2] // HOP
    rim = lax.ppermute(audio_clips, TIME, [(source, source - 1) for source in range(1, tm)])
    sequences = own_bands * CLIPS
    early = assemble(cotangent.reshape(sequences, frame_block, D), band_weight)
    parts = early.shape[1]
    early = exchange(early.reshape(sequences * parts, frame_block, D), TIME)
    early = early.reshape(tm, parts, frame_block, D)
    grads = early[:, 0].reshape(FRAMES, D)
    weight = early[:, 1:].reshape(FEAT, D)
    normed = spectrum(band_at, band_widths, audio_clips, rim, band_gain)
    feats = exchange(normed, TIME)
    factor_all = 1.0 / math.sqrt(BANDS * CLIPS * FRAMES)
    feats = pltpu.with_memory_space_constraint(feats, pltpu.VMEM)
    core = lax.axis_index("core").reshape(1)
    prepared = prepare(weight, grads, qkv_weight, out_weight)
    attended, keep, send = layer(
        core, feats, prepared, grads, norm_gain, qkv_weight, out_weight, factor_all
    )
    swap = [(0, 1), (1, 0)]
    partial = keep.astype(jnp.float32) + lax.ppermute(send, "core", swap).astype(jnp.float32)
    partial = scatter_sum(partial.astype(jnp.bfloat16), "x")
    both = jnp.concatenate(
        [attended, partial.reshape(tm, -1, D)], axis=1
    )
    both = exchange(both, TIME)
    attended_out = both[:, :frame_block].reshape(own_bands, CLIPS, frame_block, D)
    partial = gather(gather(reduced(both[:, frame_block:]), TIME), "x")
    other = lax.ppermute(partial, "core", swap)
    other = pltpu.with_memory_space_constraint(other, pltpu.VMEM)
    filled = unpack(core, partial)
    grad_qkv, grad_out = unpack(1 - core, other, filled)
    return (attended_out, grad_qkv, grad_out)


def solution(mesh):
    split = Mesh(mesh.devices.reshape(8, -1, 4, 2), TIME + BAND)
    return jax.shard_map(
        staged,
        mesh=split,
        in_specs=(
            P(None, None, TIME),
            P(),
            P(BAND, None),
            P(BAND, TIME, None),
            P(),
            P(),
            P(),
            P(BAND, None, TIME, None),
        ),
        out_specs=(P(BAND, None, TIME, None), P(), P()),
        check_vma=False,
    )
```

```python
import math

import jax
import jax.numpy as jnp
import numpy as np
from jax import lax
from jax.experimental import pallas as pl
from jax.experimental.pallas import tpu as pltpu
from jax.sharding import Mesh, PartitionSpec as P


D = 384
HEADS = 8
HDIM = 64
WIN = 2048
HOP = 441
BANDS = 64
MAXW = 128
CLIPS = 8
INNER = 512
BINS = 1024
FEAT = 512
FRAMES = 256
TIME = ("z", "y")
BAND = ("x", "core")

OUTER = 8
SPAN = WIN // OUTER
HIGH = BINS // OUTER


def window_table():
    sample_at = np.arange(WIN, dtype=np.float64)
    taper = (0.5 - 0.5 * np.cos(sample_at * (2.0 * np.pi / WIN))) / np.sqrt(WIN)
    return taper.reshape(1, WIN).astype(np.float32)


def twiddle_table():
    phase = np.outer(np.arange(OUTER), np.arange(SPAN)) % WIN
    angle = phase * (2.0 * np.pi / WIN)
    return np.concatenate([np.cos(angle), np.sin(angle)], axis=0).astype(np.float32)


def inner_table():
    phase = np.outer(np.arange(SPAN), np.arange(HIGH)) % SPAN
    angle = phase * (2.0 * np.pi / SPAN)
    real, imag = np.cos(angle), np.sin(angle)
    return np.concatenate(
        [np.concatenate([real, -imag], axis=1), np.concatenate([imag, real], axis=1)], axis=0
    ).astype(np.float32)


def rotary_table(frame_order):
    freq = np.exp(np.arange(HDIM // 2, dtype=np.float32) * np.float32(-2.0 * math.log(10000.0) / HDIM))
    angle = (frame_order.astype(np.float32)[:, None] * freq.astype(np.float32)[None, :]).astype(np.float64)
    cosine, sine = np.cos(angle), np.sin(angle)
    return (
        np.concatenate([cosine] * 4, axis=1).astype(np.float32),
        np.concatenate([-sine, sine, -sine, sine], axis=1).astype(np.float32),
    )


def split_bf16(values):
    parts = []
    for _ in range(3):
        kept = values.astype(jnp.bfloat16)
        parts.append(kept)
        values = values - kept.astype(jnp.float32)
    return parts


def one_hot(hit):
    return jnp.where(hit, 1.0, 0.0).astype(jnp.bfloat16)


def spectrum_kernel(
    place_ref,
    widths_ref,
    audio_ref,
    rim_ref,
    gain_ref,
    taper_ref,
    twiddle_ref,
    inner_ref,
    out_ref,
    lead,
    tail,
    framed,
    stage,
    bins,
    pick,
):
    own = audio_ref.shape[2]
    rows = audio_ref.shape[0] * audio_ref.shape[1]
    frames_here = own // HOP
    total = rows * frames_here
    own_bands = gain_ref.shape[0]
    for c in range(CLIPS):
        lead[2 * c : 2 * c + 2, :own] = audio_ref[c]
        tail[2 * c : 2 * c + 2, :own] = rim_ref[c]
    lane = lax.broadcasted_iota(jnp.int32, (rows, WIN), 1)
    for f in range(frames_here):
        here = own - HOP * f
        head = lead[...] if f == 0 else pltpu.roll(lead[...], WIN - HOP * f, 1)
        rest = pltpu.roll(tail[...], here % WIN, 1)
        frame = jnp.where(lane < here, head, rest) * taper_ref[...]
        for block in range(WIN // 128):
            framed[block, pl.ds(f, rows, stride=frames_here), :] = frame[
                :, block * 128 : (block + 1) * 128
            ]
    root = math.sqrt(0.5)
    for half in range(SPAN // 128):
        x = [framed[2 * n + half] for n in range(OUTER)]
        e0, e1, e2, e3 = x[0] + x[4], x[1] + x[5], x[2] + x[6], x[3] + x[7]
        d0, d1, d2, d3 = x[0] - x[4], x[1] - x[5], x[2] - x[6], x[3] - x[7]
        s02, s13 = e0 + e2, e1 + e3
        p = (d1 - d3) * root
        q = (d1 + d3) * root
        real = [s02 + s13, d0 + p, e0 - e2, d0 - p, s02 - s13]
        imag = [None, -(q + d2), e3 - e1, d2 - q, None]
        lanes = slice(half * 128, (half + 1) * 128)
        for low in range(OUTER):
            if low <= 4:
                re, im = real[low], imag[low]
            else:
                re, im = real[8 - low], -imag[8 - low]
            at = slice(low * total, (low + 1) * total)
            if low == 0:
                stage[at, half * 128 : (half + 1) * 128] = re
                stage[at, SPAN + half * 128 : SPAN + (half + 1) * 128] = jnp.zeros_like(re)
                continue
            c = twiddle_ref[low : low + 1, lanes]
            s = twiddle_ref[OUTER + low : OUTER + low + 1, lanes]
            if im is None:
                zr, zi = re * c, -(re * s)
            else:
                zr, zi = re * c + im * s, im * c - re * s
            stage[at, half * 128 : (half + 1) * 128] = zr
            stage[at, SPAN + half * 128 : SPAN + (half + 1) * 128] = zi
    made = jnp.dot(
        stage[...],
        inner_ref[...],
        preferred_element_type=jnp.float32,
        precision=lax.Precision.HIGHEST,
    )
    for low in range(OUTER):
        cols = slice(low * HIGH, (low + 1) * HIGH)
        for part in range(2):
            piece = made[low * total : (low + 1) * total, part * HIGH : (part + 1) * HIGH]
            for split, kept in enumerate(split_bf16(piece)):
                at = (split * 2 + part) * total
                bins[at : at + total, cols] = kept
    first_band = place_ref[0] * own_bands
    start = lax.fori_loop(0, first_band, lambda i, past: past + widths_ref[i], jnp.int32(0))
    within = lax.broadcasted_iota(jnp.int32, (1, MAXW), 1)
    high_at = OUTER * lax.broadcasted_iota(jnp.int32, (HIGH, MAXW), 0)
    counts = []
    for band in range(own_bands):
        width = widths_ref[first_band + band]
        target = jnp.where(within < width, start + within, -1)
        for low in range(OUTER):
            pick[low * HIGH : (low + 1) * HIGH, band * MAXW : (band + 1) * MAXW] = one_hot(
                high_at == target - low
            )
        counts.append((4 * width).astype(jnp.float32))
        start = start + width
    chosen = jnp.dot(bins[...], pick[...], preferred_element_type=jnp.float32)
    exact = chosen[: 2 * total] + chosen[2 * total : 4 * total] + chosen[4 * total :]
    feature = lax.broadcasted_iota(jnp.int32, (FEAT, FEAT), 0)
    column = lax.broadcasted_iota(jnp.int32, (FEAT, FEAT), 1)
    order = one_hot(feature == (column % MAXW) * 4 + column // MAXW)
    gain = sum(
        jnp.dot(part, order, preferred_element_type=jnp.float32)
        for part in split_bf16(gain_ref[...])
    )
    row = lax.broadcasted_iota(jnp.int32, (total, 1), 0)
    for band in range(own_bands):
        cols = slice(band * MAXW, (band + 1) * MAXW)
        re = exact[:total, cols]
        im = exact[total:, cols]
        power = jnp.sum(re * re + im * im, axis=1, keepdims=True)
        ahead = pltpu.roll(power, total - frames_here, 0)
        behind = pltpu.roll(power, frames_here, 0)
        power = power + jnp.where(row % (2 * frames_here) < frames_here, ahead, behind)
        inverse = lax.rsqrt(jnp.maximum(power / counts[band], 0.25))
        for r in range(2):
            value = ((re, im)[r] * inverse).reshape(CLIPS, 2 * frames_here, MAXW)
            for a in range(2):
                which = 2 * a + r
                lanes = slice(which * MAXW, (which + 1) * MAXW)
                own_gain = gain[band : band + 1, lanes]
                out_ref[band * CLIPS : (band + 1) * CLIPS, :, lanes] = (
                    value[:, a * frames_here : (a + 1) * frames_here, :] * own_gain[None]
                ).astype(jnp.bfloat16)


def assemble_kernel(grads_ref, weight_ref, out_ref):
    block = grads_ref.shape[1]
    steps = weight_ref.shape[1] // block
    out_ref[:, 0] = grads_ref[...]
    for band in range(weight_ref.shape[0]):
        for step in range(steps):
            piece = weight_ref[band, step * block : (step + 1) * block, :]
            for c in range(CLIPS):
                out_ref[band * CLIPS + c, 1 + step] = piece


def dot(left, right, dims=((1,), (0,))):
    return lax.dot_general(left, right, (dims, ((), ())), preferred_element_type=jnp.float32)


def split_heads(values):
    low = lax.broadcasted_iota(jnp.int32, values.shape, 1) < HDIM
    return (
        jnp.where(low, values, 0.0).astype(jnp.bfloat16),
        jnp.where(low, 0.0, values).astype(jnp.bfloat16),
    )


def prepare_kernel(weight_ref, grads_ref, qkv_ref, outw_ref, embed_ref, heads_ref, turned_ref):
    natural = lax.broadcasted_iota(jnp.int32, (FEAT, FEAT), 1)
    wanted = lax.broadcasted_iota(jnp.int32, (FEAT, FEAT), 0)
    order = one_hot(natural == (wanted % MAXW) * 4 + wanted // MAXW)
    embed_ref[...] = dot(order, weight_ref[...]).astype(jnp.bfloat16)
    grad_mixed = dot(grads_ref[...], outw_ref[...], ((1,), (1,)))
    for pair in range(HEADS // 2):
        low, high = split_heads(grad_mixed[:, pair * 128 : (pair + 1) * 128])
        heads_ref[pair, :FRAMES, :] = low
        heads_ref[pair, FRAMES:, :] = high
    row = lax.broadcasted_iota(jnp.int32, (128, 128), 0)
    lane = lax.broadcasted_iota(jnp.int32, (128, 128), 1)
    swap = one_hot(row == lane + jnp.where(lane % HDIM < HDIM // 2, HDIM // 2, -(HDIM // 2)))
    for part in range(2):
        for pair in range(HEADS // 2):
            piece = qkv_ref[:, part * INNER + pair * 128 : part * INNER + (pair + 1) * 128]
            at = pair * 512 + part * 256
            turned_ref[:, at : at + 128] = piece
            turned_ref[:, at + 128 : at + 256] = dot(piece, swap).astype(jnp.bfloat16)


def layer_kernel(
    core_ref,
    embed_ref,
    gain_ref,
    feats_ref,
    turned_hbm,
    qkv_hbm,
    cos_hbm,
    sin_hbm,
    heads_hbm,
    outw_hbm,
    grads_hbm,
    attended_ref,
    keep_ref,
    send_ref,
    turned_ref,
    plain_ref,
    cos_ref,
    sin_ref,
    heads_ref,
    outw_ref,
    grads_ref,
    mixed_s,
    gproj_s,
    halves,
    sems,
    *,
    factor_all,
):
    pairs = (
        (turned_hbm, turned_ref),
        (qkv_hbm.at[:, 2 * INNER :], plain_ref),
        (cos_hbm, cos_ref),
        (sin_hbm, sin_ref),
        (heads_hbm, heads_ref),
        (outw_hbm, outw_ref),
        (grads_hbm, grads_ref),
    )
    copies = [
        pltpu.make_async_copy(source, target, sems.at[at])
        for at, (source, target) in enumerate(pairs)
    ]
    for copy in copies:
        copy.start()
    x = dot(feats_ref[...].reshape(FRAMES, FEAT), embed_ref[...]).astype(jnp.bfloat16).astype(jnp.float32)
    scale = lax.rsqrt(jnp.mean(x * x, axis=1, keepdims=True) + 1e-06)
    normed_x = (x * scale * gain_ref[...]).astype(jnp.bfloat16)
    for copy in copies:
        copy.wait()
    factor = 1.0 / math.sqrt(HDIM)
    cosine = cos_ref[...]
    sine = sin_ref[...]
    values = dot(normed_x, plain_ref[...])

    def opened(pair):
        made = dot(normed_x, turned_ref[:, pair * 512 : (pair + 1) * 512])
        q, q_swap, k, k_swap = (made[:, at * 128 : (at + 1) * 128] for at in range(4))
        v = values[:, pair * 128 : (pair + 1) * 128]
        query = split_heads((q * cosine + q_swap * sine) * factor)
        query_swap = split_heads((q_swap * cosine - q * sine) * factor)
        turned = k * cosine + k_swap * sine
        key = split_heads(turned)
        key_swap = split_heads(k_swap * cosine - k * sine)
        value = split_heads(v)
        stacked = jnp.concatenate(query, axis=0)
        scores = dot(stacked, turned.astype(jnp.bfloat16), ((1,), (1,)))
        grad_p = dot(heads_ref[pair], v.astype(jnp.bfloat16), ((1,), (1,)))
        both_q = jnp.concatenate([stacked, jnp.concatenate(query_swap, axis=0)], axis=1)
        both_k = [jnp.concatenate([a, b], axis=1) for a, b in zip(key, key_swap)]
        return scores, grad_p, both_q, both_k, value

    def closed(pair, scores, grad_p, both_q, both_k, value):
        cols = slice(pair * 128, (pair + 1) * 128)
        peak = jnp.max(scores, axis=1, keepdims=True)
        expo = jnp.exp(scores - peak)
        probs = expo / jnp.sum(expo, axis=1, keepdims=True)
        probs_b = probs.astype(jnp.bfloat16)
        row_dot = jnp.sum(probs * grad_p, axis=1, keepdims=True)
        grad_s = (probs * (grad_p - row_dot)).astype(jnp.bfloat16)
        mixed = dot(probs_b[:FRAMES], value[0]) + dot(probs_b[FRAMES:], value[1])
        grad_v = dot(probs_b, heads_ref[pair], ((0,), (0,)))
        grad_q = (dot(grad_s[:FRAMES], both_k[0]) + dot(grad_s[FRAMES:], both_k[1])) * factor
        grad_k = dot(grad_s, both_q, ((0,), (0,)))
        mixed_s[:, cols] = mixed.astype(jnp.bfloat16)
        for part, grad in enumerate((grad_q, grad_k)):
            turned = grad[:, :128] * cosine - grad[:, 128:] * sine
            gproj_s[:, part * INNER + pair * 128 : part * INNER + (pair + 1) * 128] = turned.astype(
                jnp.bfloat16
            )
        gproj_s[:, 2 * INNER + pair * 128 : 2 * INNER + (pair + 1) * 128] = grad_v.astype(
            jnp.bfloat16
        )

    ready = opened(0)
    for pair in range(HEADS // 2):
        following = opened(pair + 1) if pair + 1 < HEADS // 2 else None
        closed(pair, *ready)
        ready = following
    mixed_b = mixed_s[...]
    attended = x + dot(mixed_b, outw_ref[...])
    attended_ref[...] = attended.reshape(attended_ref.shape).astype(jnp.bfloat16)
    core = core_ref[0]

    def place(first, values):
        values = (values * factor_all).astype(jnp.bfloat16)
        rows = values.shape[0] // 2
        halves[core, first : first + rows, :] = values[:rows]
        halves[1 - core, first : first + rows, :] = values[rows:]

    for block in range(3 * INNER // D):
        place(
            block * D // 2, dot(normed_x, gproj_s[:, block * D : (block + 1) * D], ((0,), (0,)))
        )
    place(3 * INNER // 2, dot(mixed_b, grads_ref[...], ((0,), (0,))))
    keep_ref[...] = halves[0]
    send_ref[...] = halves[1]


def unpack_kernel(core_ref, half_ref, *refs):
    grad_qkv_hbm, grad_out_hbm, wide_ref, out_sems = refs[-4:]
    core = core_ref[0]
    rows = D // 2
    spans = [(at * rows, rows) for at in range(3 * INNER // D)] + [(3 * INNER // 2, INNER // 2)]
    leaving = []
    for at, (first, count) in enumerate(spans):
        span = slice(first, first + count)
        wide_ref[span, :] = half_ref[span, :].astype(jnp.float32)
        place = pl.ds(pl.multiple_of(core * count, count), count)
        if at < len(spans) - 1:
            target = grad_qkv_hbm.at[place, pl.ds(at * D, D)]
        else:
            target = grad_out_hbm.at[place, :]
        leaving.append(
            pltpu.make_async_copy(wide_ref.at[pl.ds(first, count), :], target, out_sems.at[at])
        )
        leaving[-1].start()
    for copy in leaving:
        copy.wait()


def in_vmem(values):
    return pltpu.with_memory_space_constraint(values, pltpu.VMEM)


def whole(memory_space=pltpu.VMEM):
    return pl.BlockSpec(memory_space=memory_space)


def spectrum(band_at, band_widths, audio, rim, gain):
    rows, own = audio.shape[0] * audio.shape[1], audio.shape[2]
    frames_here = own // HOP
    total = rows * frames_here
    own_bands = gain.shape[0]
    return pl.pallas_call(
        spectrum_kernel,
        out_shape=jax.ShapeDtypeStruct((own_bands * CLIPS, frames_here, FEAT), jnp.bfloat16),
        in_specs=[whole(pltpu.SMEM)] * 2 + [whole()] * 6,
        out_specs=whole(),
        scratch_shapes=[
            pltpu.VMEM((rows, WIN), jnp.float32),
            pltpu.VMEM((rows, WIN), jnp.float32),
            pltpu.VMEM((WIN // 128, total, 128), jnp.float32),
            pltpu.VMEM((OUTER * total, 2 * SPAN), jnp.float32),
            pltpu.VMEM((6 * total, BINS), jnp.bfloat16),
            pltpu.VMEM((BINS, own_bands * MAXW), jnp.bfloat16),
        ],
        name="spectrum",
    )(
        band_at.reshape(1),
        band_widths,
        audio,
        rim,
        gain,
        jnp.asarray(window_table()),
        jnp.asarray(twiddle_table()),
        jnp.asarray(inner_table()),
    )


def assemble(grads, weight):
    sequences, block, width = grads.shape
    return pl.pallas_call(
        assemble_kernel,
        out_shape=jax.ShapeDtypeStruct(
            (sequences, 1 + weight.shape[1] // block, block, width), grads.dtype
        ),
        in_specs=[whole()] * 2,
        out_specs=whole(),
        name="assemble",
    )(grads, weight)


def prepare(weight, grads, qkv_weight, out_weight):
    return pl.pallas_call(
        prepare_kernel,
        out_shape=(
            pltpu.VMEM((FEAT, D), jnp.bfloat16),
            jax.ShapeDtypeStruct((HEADS // 2, 2 * FRAMES, 128), jnp.bfloat16),
            jax.ShapeDtypeStruct((D, 4 * INNER), jnp.bfloat16),
        ),
        in_specs=[whole()] * 4,
        out_specs=(whole(),) * 3,
        name="prepare",
    )(weight, grads, qkv_weight, out_weight)


def layer(core, feats, prepared, grads, norm_gain, qkv_weight, out_weight, factor_all):
    embed, heads, turned = prepared
    cosine, sine = rotary_table(np.arange(FRAMES))
    later = (
        turned,
        qkv_weight,
        jnp.asarray(cosine),
        jnp.asarray(sine),
        heads,
        out_weight,
        grads,
    )
    return pl.pallas_call(
        lambda *refs: layer_kernel(*refs, factor_all=factor_all),
        out_shape=(
            pltpu.VMEM(feats.shape[:2] + (D,), jnp.bfloat16),
            pltpu.VMEM((2 * INNER, D), jnp.bfloat16),
            pltpu.VMEM((2 * INNER, D), jnp.bfloat16),
        ),
        in_specs=[whole(pltpu.SMEM)] + [whole()] * 3 + [whole(pl.ANY)] * len(later),
        out_specs=(whole(),) * 3,
        scratch_shapes=[
            pltpu.VMEM((D, INNER) if value is qkv_weight else value.shape, value.dtype)
            for value in later
        ]
        + [
            pltpu.VMEM((FRAMES, INNER), jnp.bfloat16),
            pltpu.VMEM((FRAMES, 3 * INNER), jnp.bfloat16),
            pltpu.VMEM((2, 2 * INNER, D), jnp.bfloat16),
            pltpu.SemaphoreType.DMA((len(later),)),
        ],
        name="layer",
    )(core, in_vmem(embed), norm_gain.reshape(1, D), in_vmem(feats), *later)


def unpack(core, half, filled=()):
    return pl.pallas_call(
        unpack_kernel,
        out_shape=(
            jax.ShapeDtypeStruct((D, 3 * INNER), jnp.float32),
            jax.ShapeDtypeStruct((INNER, D), jnp.float32),
        ),
        in_specs=[whole(pltpu.SMEM), whole()] + [whole(pl.ANY)] * len(filled),
        out_specs=(whole(pl.ANY),) * 2,
        input_output_aliases={2 + at: at for at in range(len(filled))},
        scratch_shapes=[
            pltpu.VMEM(half.shape, jnp.float32),
            pltpu.SemaphoreType.DMA((3 * INNER // D + 1,)),
        ],
        name="unpack",
    )(core, in_vmem(half), *filled)


def exchange(blocks, axis):
    return lax.all_to_all(blocks, axis, split_axis=0, concat_axis=0, tiled=True)


def reduced(blocks):
    return jnp.sum(blocks.astype(jnp.float32), axis=0).astype(jnp.bfloat16)


def scatter_sum(values, axis):
    count = lax.axis_size(axis)
    blocks = values.reshape(count, values.shape[0] // count, values.shape[1])
    return reduced(exchange(blocks, axis))


def gather(values, axis):
    count = lax.axis_size(axis)
    blocks = jnp.broadcast_to(values[None], (count,) + values.shape)
    return exchange(blocks, axis).reshape(count * values.shape[0], values.shape[1])


def staged(
    audio_clips, band_widths, band_gain, band_weight, norm_gain, qkv_weight, out_weight, cotangent
):
    tm = lax.axis_size(TIME)
    band_at = lax.axis_index("x") * lax.axis_size("core") + lax.axis_index("core")
    own_bands = band_gain.shape[0]
    frame_block = audio_clips.shape[2] // HOP
    rim = lax.ppermute(audio_clips, TIME, [(source, source - 1) for source in range(1, tm)])
    sequences = own_bands * CLIPS
    early = assemble(cotangent.reshape(sequences, frame_block, D), band_weight)
    parts = early.shape[1]
    early = exchange(early.reshape(sequences * parts, frame_block, D), TIME)
    early = early.reshape(tm, parts, frame_block, D)
    grads = early[:, 0].reshape(FRAMES, D)
    weight = early[:, 1:].reshape(FEAT, D)
    normed = spectrum(band_at, band_widths, audio_clips, rim, band_gain)
    feats = exchange(normed, TIME)
    factor_all = 1.0 / math.sqrt(BANDS * CLIPS * FRAMES)
    core = lax.axis_index("core").reshape(1)
    prepared = prepare(weight, grads, qkv_weight, out_weight)
    attended, keep, send = layer(
        core, feats, prepared, grads, norm_gain, qkv_weight, out_weight, factor_all
    )
    swap = [(0, 1), (1, 0)]
    partial = keep.astype(jnp.float32) + lax.ppermute(send, "core", swap).astype(jnp.float32)
    partial = scatter_sum(partial.astype(jnp.bfloat16), "x")
    both = jnp.concatenate(
        [attended, partial.reshape(tm, -1, D)], axis=1
    )
    both = exchange(both, TIME)
    attended_out = both[:, :frame_block].reshape(own_bands, CLIPS, frame_block, D)
    partial = gather(gather(reduced(both[:, frame_block:]), TIME), "x")
    other = lax.ppermute(partial, "core", swap)
    filled = unpack(core, partial)
    grad_qkv, grad_out = unpack(1 - core, other, filled)
    return (attended_out, grad_qkv, grad_out)


def solution(mesh):
    split = Mesh(mesh.devices.reshape(8, -1, 4, 2), TIME + BAND)
    return jax.shard_map(
        staged,
        mesh=split,
        in_specs=(
            P(None, None, TIME),
            P(),
            P(BAND, None),
            P(BAND, TIME, None),
            P(),
            P(),
            P(),
            P(BAND, None, TIME, None),
        ),
        out_specs=(P(BAND, None, TIME, None), P(), P()),
        check_vma=False,
    )
```
